512 devices in a mesh: coil: 8 (over z), slab: 64 (over y, x, core).
Axes of the slice: x: 4, y: 8, z: 8, core: 2. Of those that a mesh axis runs over, the one named last changes fastest.
Arguments:
- solution: float32 [2, 1, 128, 192, 256], P(None, None, 'slab', 'coil'), may hold values from -6 to 6
- residual: float32 [2, 1, 128, 192, 256], P(None, None, 'slab', 'coil'), may hold values from -6 to 6
- direction: float32 [2, 1, 128, 192, 256], P(None, None, 'slab', 'coil'), may hold values from -6 to 6
- sens_maps: float32 [2, 16, 128, 192, 256], P(None, 'coil', 'slab'), may hold values from -1.05 to 1.05
- sampling: int32 [1, 128, 192], replicated, may hold values from 0 to 1, as said below
Outputs:
- next_solution: float32 [2, 1, 128, 192, 256], P(None, None, 'slab', 'coil')
- next_residual: float32 [2, 1, 128, 192, 256], P(None, None, 'slab', 'coil')
- next_direction: float32 [2, 1, 128, 192, 256], P(None, None, 'slab', 'coil')
The draws below stay inside these ranges and needn't reach their ends.
Inputs may be any that keep to these rules, and one draw needn't show every extreme that they name: sampling is 1 on every line whose kx lies within 4 of 0 or of 128 and whose ky lies within 4 of 0 or of 192.
All inputs are finite; a program needn't handle non-finite values.
Results may differ from the reference program's by a relative error of at most 0.00016.
Values sent between devices are 32-bit elements; how exact they have to be, the bound alone decides.
No kernel may reach another device: no remote copies, remote signals or barrier semaphores. Data moves between devices by JAX's collectives and lax.ppermute only.
A program may use at most 64 MiB of HBM per device.

```python
import math
import jax
import jax.numpy as jnp
from jax import lax

NX = 128
NY = 192
NZ = 256
COILS = 16
FRAMES = 1
CALIB = 4


def smooth_factor(key, length, count):
    first_key, second_key = jax.random.split(key)
    weights = jax.random.uniform(first_key, (count, 3), jnp.float32, -1.0, 1.0)
    phases = jax.random.uniform(second_key, (count, 3), jnp.float32, -math.pi, math.pi)
    position = jnp.arange(length, dtype=jnp.float32) / length
    frequency = jnp.arange(3, dtype=jnp.float32)
    angles = 2.0 * math.pi * frequency[None, :, None] * position[None, None, :] + phases[:, :, None]
    profile = jnp.sum(weights[:, :, None] * jnp.cos(angles), axis=1)
    largest = jnp.maximum(jnp.max(jnp.abs(profile), axis=1, keepdims=True), 0.05)
    return profile / largest


def direction_parts(key):
    base_key = jax.random.fold_in(key, 11)
    x_key, y_key, scale_key, noise_key = jax.random.split(base_key, 4)
    along_x = smooth_factor(x_key, NX, 2 * FRAMES).reshape(2, FRAMES, NX)
    along_y = smooth_factor(y_key, NY, 2 * FRAMES).reshape(2, FRAMES, NY)
    smooth = 2.5 * along_x[:, :, :, None, None] * along_y[:, :, None, :, None]
    exponent = jax.random.uniform(scale_key, (1, FRAMES, 1, 1, NZ), jnp.float32, math.log(0.25), math.log(2.5))
    noise_part = jax.random.normal(noise_key, (2, FRAMES, NX, NY, NZ), jnp.float32)
    amplitude = jnp.exp(exponent)
    return jnp.clip(amplitude * smooth + noise_part, -6.0, 6.0)


def draw_direction(key, part):
    return direction_parts(key)


def draw_residual(key, part):
    searched = direction_parts(key)
    noise_key = jax.random.fold_in(key, 29)
    noise_part = jax.random.normal(noise_key, (2, FRAMES, NX, NY, NZ), jnp.float32)
    return jnp.clip(0.8 * searched + 0.6 * noise_part, -6.0, 6.0)


def draw_sens_maps(key, part):
    base_key = jax.random.fold_in(key, 23)
    x_key, y_key, rough_key = jax.random.split(base_key, 3)
    along_x = smooth_factor(x_key, NX, 2 * COILS).reshape(2, COILS, NX)
    along_y = smooth_factor(y_key, NY, 2 * COILS).reshape(2, COILS, NY)
    rough_factor = jax.random.uniform(rough_key, (1, COILS, NX, NY, NZ), jnp.float32, 0.5, 1.5)
    return 0.65 * along_x[:, :, :, None, None] * along_y[:, :, None, :, None] * rough_factor


def draw_sampling(key, part):
    base_key = jax.random.fold_in(key, 37)
    chosen = jax.random.randint(base_key, (FRAMES, NX, NY), 0, 3)
    index_x = jnp.arange(NX, dtype=jnp.int32)
    index_y = jnp.arange(NY, dtype=jnp.int32)
    near_x = (index_x <= CALIB) | (index_x >= NX - CALIB)
    near_y = (index_y <= CALIB) | (index_y >= NY - CALIB)
    centre = near_x[:, None] & near_y[None, :]
    return jnp.where(centre[None] | (chosen == 0), 1, 0).astype(jnp.int32)


def shard_levels(own_key, extent, cuts, low, top_value):
    level, own = 1.0, jax.random.fold_in(own_key, 6)
    for dim, parts in cuts:
        draws = jnp.exp(jax.random.uniform(jax.random.fold_in(own, dim), (parts,), jnp.float32, low / len(cuts), top_value / len(cuts)))
        level = level * jnp.repeat(draws, extent[dim] // parts).reshape([-1 if axis == dim else 1 for axis in range(len(extent))])
    return level


def scatter_about(stream_key, extent, width, most, shards=(), held_as=jnp.bfloat16):
    drawn = width * jax.random.normal(stream_key, extent, jnp.float32)
    if shards:
        drawn = drawn * shard_levels(stream_key, extent, shards, -0.22, 0.18)
    return jnp.clip(drawn, -most, most).astype(held_as)


def setup_inputs(seed: int = 0) -> dict:
    arg_keys = jax.random.split(jax.random.key(seed), 6)
    return {
        "solution": scatter_about(arg_keys[0], (2, FRAMES, NX, NY, NZ), 1.0, 6.0, ((2, 64), (3, 8)), jnp.float32),
        "residual": draw_residual(jax.random.fold_in(arg_keys[5], 71), 0),
        "direction": draw_direction(jax.random.fold_in(arg_keys[5], 71), 0),
        "sens_maps": draw_sens_maps(jax.random.fold_in(arg_keys[5], 71), 0),
        "sampling": draw_sampling(jax.random.fold_in(arg_keys[5], 71), 0),
    }


damping_weight = 0.5


def normal_map(direction, sens_maps, sampling):
    field = lax.complex(direction[0], direction[1])
    weight = sampling.astype(direction.dtype)[:, :, :, None]

    def add_coil(total, maps):
        coil = lax.complex(maps[0], maps[1])
        spectra = jnp.fft.fft2(coil[None] * field, axes=(1, 2), norm="ortho")
        back = jnp.fft.ifft2(spectra * weight, axes=(1, 2), norm="ortho")
        term = jnp.conj(coil)[None] * back
        return total + jnp.stack([jnp.real(term), jnp.imag(term)]), None

    total, unused = lax.scan(add_coil, jnp.zeros_like(direction), jnp.moveaxis(sens_maps, 1, 0))
    return total + damping_weight * direction


def reference(solution, residual, direction, sens_maps, sampling):
    image_ap = normal_map(direction, sens_maps, sampling)
    norm_now = jnp.sum(residual * residual)
    curvature = jnp.sum(direction * image_ap)
    alpha = norm_now / curvature
    next_solution = solution + alpha * direction
    next_residual = residual - alpha * image_ap
    fresh = jnp.sum(next_residual * next_residual)
    next_direction = next_residual + (fresh / norm_now) * direction
    return next_solution, next_residual, next_direction
```

```python
import math

import jax
import jax.numpy as jnp
import ml_dtypes
import numpy as np
from jax import lax
from jax.experimental import pallas as pl
from jax.experimental.pallas import tpu as pltpu
from jax.sharding import PartitionSpec as P

damping_weight = 0.5

LANES = 128
ROWS = 8
MESSAGE_D = 6
MESSAGE_R = 7
HALF = 64
SUMS_AT = 48


def split_pair(table):
    high = table.astype(ml_dtypes.bfloat16)
    low = (table - high.astype(np.float64)).astype(ml_dtypes.bfloat16)
    return np.stack([high, low])


def angles(length):
    index = np.arange(length)
    angle = (index[:, None] * index[None, :] % length) * (2.0 * math.pi / length)
    scale = 1.0 / math.sqrt(length)
    return np.cos(angle) * scale, np.sin(angle) * scale


def make_tables(size_x, size_y):
    cos_y, sin_y = angles(size_y)
    cos_x, sin_x = angles(size_x)
    re_from_re = np.concatenate([cos_y[:, :LANES], -sin_y[:, :LANES], cos_y[:, LANES:], -sin_y[:, LANES:]], axis=1)
    re_from_im = np.concatenate([sin_y[:, :LANES], cos_y[:, :LANES], sin_y[:, LANES:], cos_y[:, LANES:]], axis=1)
    fwd_y = np.zeros((2, 4 * LANES, 3 * LANES))
    for row in range(2):
        for part, block in enumerate((re_from_re, re_from_im)):
            base = part * 2 * LANES
            fwd_y[row, base : base + LANES] = block[:LANES]
            high = base + LANES + row * HALF
            fwd_y[row, high : high + HALF] = block[LANES:]
    to_re = np.concatenate([cos_y[:LANES], -sin_y[:LANES], cos_y[LANES:], -sin_y[LANES:]], axis=0)
    to_im = np.concatenate([sin_y[:LANES], cos_y[:LANES], sin_y[LANES:], cos_y[LANES:]], axis=0)
    inv_low = np.concatenate([to_re[:, :LANES], to_im[:, :LANES]], axis=1)
    inv_high = np.zeros((2, 3 * LANES, 2 * LANES))
    for row in range(2):
        inv_high[row, :, row * HALF : (row + 1) * HALF] = to_re[:, LANES:]
        inv_high[row, :, LANES + row * HALF : LANES + (row + 1) * HALF] = to_im[:, LANES:]
    order = np.concatenate([np.arange(0, size_x, 2), np.arange(1, size_x, 2)])
    fwd_x = np.concatenate([cos_x[:, order], sin_x[:, order]], axis=0)
    inv_x = np.concatenate([cos_x[order], sin_x[order]], axis=0)
    return [split_pair(t) for t in (fwd_y, fwd_x, inv_x, inv_low, inv_high)]


def pack_kernel(maps_ref, direction_ref, residual_ref, out_ref):
    cells = maps_ref.shape[4]

    def put(core, slot, block):
        out_ref[pl.ds(core * ROWS + slot, cells, stride=2 * ROWS), :] = block.T

    for core in range(2):
        for part in range(2):
            for row in range(2):
                put(core, part * 2 + row, maps_ref[part, core, row, :LANES, :])
            put(
                core,
                4 + part,
                jnp.concatenate([maps_ref[part, core, 0, LANES:, :], maps_ref[part, core, 1, LANES:, :]], axis=0),
            )
    own = direction_ref.shape[3]
    pieces = [direction_ref[part, 0, row] for part in range(2) for row in range(2)]
    filler = jnp.zeros((LANES - 4 * own, cells), jnp.float32)
    field = jnp.concatenate(pieces + [filler], axis=0)
    for core in range(2):
        put(core, MESSAGE_D, field)
        filler = jnp.zeros((LANES - 2 * own, cells), jnp.float32)
        put(core, MESSAGE_R, jnp.concatenate([residual_ref[core, 0, 0], residual_ref[core, 0, 1], filler], axis=0))


def lane_index(rows):
    return lax.broadcasted_iota(jnp.int32, (rows, LANES), 1)


def spread(blocks, own, slots):
    lane = lane_index(HALF)
    result = []
    for slot in slots:
        low = jnp.zeros((HALF, LANES), jnp.float32)
        high = jnp.zeros((HALF, LANES), jnp.float32)
        for c, block in enumerate(blocks):
            start = c * own
            moved = pltpu.roll(block, (start - slot * own) % LANES, 1)
            if start < LANES:
                low = jnp.where((lane >= start) & (lane < start + own), moved, low)
            if start + own > LANES:
                at = start - LANES
                high = jnp.where((lane >= at) & (lane < at + own), moved, high)
        result.append((low, high))
    return result


def join_high(first, second):
    return jnp.where(lane_index(HALF) < HALF, first, pltpu.roll(second, HALF, 1))


def halves(value):
    high = value.astype(jnp.bfloat16)
    low = (value - high.astype(jnp.float32)).astype(jnp.bfloat16)
    return high, low


def dot3(left_high, left_low, right_high, right_low):
    def dot(a, b):
        return jnp.dot(a, b, preferred_element_type=jnp.float32)

    return dot(left_high, right_high) + (dot(left_high, right_low) + dot(left_low, right_high))


def normal_kernel(
    core_ref,
    recv_ref,
    weight_ref,
    fwd_y_ref,
    fwd_x_ref,
    inv_x_ref,
    inv_low_ref,
    inv_high_ref,
    own_ref,
    send_ref,
    field_ref,
    line_ref,
    mid_ref,
    back_ref,
    total_ref,
    image_ref,
):
    coils = recv_ref.shape[0] // (ROWS * HALF)
    own = 2 * 96 // coils

    def load(c, slot):
        return recv_ref[pl.ds(c * HALF * ROWS + slot, HALF, stride=ROWS), :]

    pieces = spread([load(c, MESSAGE_D) for c in range(coils)], own, range(4))
    for part in range(2):
        (low0, high0), (low1, high1) = pieces[2 * part], pieces[2 * part + 1]
        image_ref[part, 0] = low0
        image_ref[part, 1] = low1
        image_ref[part, 2] = join_high(high0, high1)
    for c in range(coils):
        rows = pl.ds(c * HALF, HALF)
        for slot in range(3):
            s_re = load(c, slot if slot < 2 else 4)
            s_im = load(c, slot + 2 if slot < 2 else 5)
            d_re, d_im = image_ref[0, slot], image_ref[1, slot]
            for part, value in enumerate((s_re * d_re - s_im * d_im, s_re * d_im + s_im * d_re)):
                base = part * 2 * LANES
                for term, half in enumerate(halves(value)):
                    if slot < 2:
                        line_ref[term, slot, rows, base : base + LANES] = half
                    else:
                        for row in range(2):
                            line_ref[term, row, rows, base + LANES : base + 2 * LANES] = half
    for row in range(2):
        spectra = dot3(line_ref[0, row], line_ref[1, row], fwd_y_ref[0, row], fwd_y_ref[1, row])
        for term, half in enumerate(halves(spectra)):
            for c in range(coils):
                mid_ref[term, c, row * HALF : (row + 1) * HALF, :] = half[c * HALF : (c + 1) * HALF]
    weight_low = weight_ref[:, :LANES].astype(jnp.float32)
    weight_high = weight_ref[:, LANES:].astype(jnp.float32)
    weight_mix = jnp.concatenate([weight_high, weight_high], axis=1)
    sign = jnp.where(lane_index(LANES) < HALF, 1.0, -1.0).astype(jnp.float32)
    for c in range(coils):
        both = dot3(fwd_x_ref[0], fwd_x_ref[1], mid_ref[0, c], mid_ref[1, c])
        p, q = both[:LANES], both[LANES:]
        turned = sign * pltpu.roll(q[:, 2 * LANES :], HALF, 1)
        masked = jnp.concatenate(
            [
                (p[:, :LANES] + q[:, LANES : 2 * LANES]) * weight_low,
                (p[:, LANES : 2 * LANES] - q[:, :LANES]) * weight_low,
                (p[:, 2 * LANES :] + turned) * weight_mix,
            ],
            axis=1,
        )
        masked_high, masked_low = halves(masked)
        both = dot3(inv_x_ref[0], inv_x_ref[1], masked_high, masked_low)
        p, q = both[:LANES], both[LANES:]
        turned = sign * pltpu.roll(q[:, 2 * LANES :], HALF, 1)
        columns = (
            p[:, :LANES] - q[:, LANES : 2 * LANES],
            p[:, LANES : 2 * LANES] + q[:, :LANES],
            p[:, 2 * LANES :] - turned,
        )
        for group, value in enumerate(columns):
            for term, half in enumerate(halves(value)):
                for row in range(2):
                    back_ref[term, row, c * HALF : (c + 1) * HALF, group * LANES : (group + 1) * LANES] = half[
                        row * HALF : (row + 1) * HALF
                    ]
    for slot in range(3):
        if slot < 2:
            value = dot3(back_ref[0, slot], back_ref[1, slot], inv_low_ref[0], inv_low_ref[1])
        else:
            value = dot3(back_ref[0, 0], back_ref[1, 0], inv_high_ref[0, 0], inv_high_ref[1, 0]) + dot3(
                back_ref[0, 1], back_ref[1, 1], inv_high_ref[0, 1], inv_high_ref[1, 1]
            )
        sum_re = jnp.zeros((HALF, LANES), jnp.float32)
        sum_im = jnp.zeros((HALF, LANES), jnp.float32)
        for c in range(coils):
            s_re = load(c, slot if slot < 2 else 4)
            s_im = load(c, slot + 2 if slot < 2 else 5)
            y_re = value[c * HALF : (c + 1) * HALF, :LANES]
            y_im = value[c * HALF : (c + 1) * HALF, LANES:]
            sum_re = sum_re + (s_re * y_re + s_im * y_im)
            sum_im = sum_im + (s_re * y_im - s_im * y_re)
        total_ref[0, slot] = sum_re
        total_ref[1, slot] = sum_im
    core = core_ref[0]
    own_ref[...] = total_ref[core]
    send_ref[...] = total_ref[1 - core]
    field_ref[0] = image_ref[core]
    pieces = spread([load(c, MESSAGE_R) for c in range(coils)], own, range(2))
    field_ref[1, 0] = pieces[0][0]
    field_ref[1, 1] = pieces[1][0]
    field_ref[1, 2] = join_high(pieces[0][1], pieces[1][1])


def finish_kernel(own_ref, other_ref, field_ref, out_ref):
    direction = field_ref[0]
    residual = field_ref[1]
    image_ap = own_ref[...] + other_ref[...] + damping_weight * direction
    lane = lane_index(HALF)
    coils = out_ref.shape[0] // HALF
    own = 2 * 96 // coils
    sums = jnp.zeros((HALF, LANES), jnp.float32)
    products = (residual * residual, direction * image_ap, residual * image_ap, image_ap * image_ap)
    for index, product in enumerate(products):
        sums = jnp.where(lane == SUMS_AT + index, jnp.sum(product), sums)
    high = image_ap[2]
    for c in range(coils):
        start = c * own
        block = sums
        for row in range(2):
            at = row * own
            inside = (lane >= at) & (lane < at + own)
            if start < LANES:
                block = jnp.where(inside, pltpu.roll(image_ap[row], (at - start) % LANES, 1), block)
            if start + own > LANES:
                moved = pltpu.roll(high, (at - (start - LANES + row * HALF)) % LANES, 1)
                if start < LANES:
                    inside = inside & (lane >= at + LANES - start)
                block = jnp.where(inside, moved, block)
        out_ref[c * HALF : (c + 1) * HALF, :] = block


def update_kernel(
    recv_ref, solution_ref, residual_ref, direction_ref, next_solution_ref, next_residual_ref, next_direction_ref
):
    cells = recv_ref.shape[0] // 2
    own = direction_ref.shape[3]
    totals = jnp.sum(recv_ref[...], axis=0, keepdims=True)
    lane = lax.broadcasted_iota(jnp.int32, (1, LANES), 1)

    def pick(index):
        return jnp.sum(jnp.where(lane == SUMS_AT + index, totals, 0.0), axis=1, keepdims=True)

    norm_now, curvature, cross, square = pick(0), pick(1), pick(2), pick(3)
    alpha = norm_now / curvature
    fresh = jnp.maximum(norm_now + alpha * (alpha * square - 2.0 * cross), 0.0)
    beta = fresh / norm_now
    for part in range(2):
        turned = recv_ref[pl.ds(part, cells, stride=2), :].T
        for row in range(2):
            image_ap = turned[row * own : (row + 1) * own]
            direction = direction_ref[part, 0, row]
            next_residual = residual_ref[part, 0, row] - alpha * image_ap
            next_solution_ref[part, 0, row] = solution_ref[part, 0, row] + alpha * direction
            next_residual_ref[part, 0, row] = next_residual
            next_direction_ref[part, 0, row] = next_residual + beta * direction


def body(solution, residual, direction, sens_maps, sampling):
    axes = ("coil", "slab")
    devices = lax.axis_size(axes)
    planes = lax.axis_size("coil")
    f32 = jnp.float32
    params = pltpu.CompilerParams(vmem_limit_bytes=48 * 1024 * 1024)
    packed = pl.pallas_call(
        pack_kernel,
        out_shape=jax.ShapeDtypeStruct((devices * ROWS, LANES), f32),
        compiler_params=params,
        name="pack",
    )(sens_maps, direction, residual)
    moved = lax.all_to_all(packed.reshape(devices, ROWS, LANES), axes, 0, 0, tiled=True)
    tables = [jnp.asarray(t) for t in make_tables(sampling.shape[1], sampling.shape[2])]
    core = (lax.axis_index("slab") % 2).astype(jnp.int32).reshape(1)
    lines = planes * HALF
    bf16 = jnp.bfloat16
    whole = pl.BlockSpec(memory_space=pltpu.VMEM)
    part = jax.ShapeDtypeStruct((3, HALF, LANES), f32)
    own, send, field = pl.pallas_call(
        normal_kernel,
        in_specs=[pl.BlockSpec(memory_space=pltpu.SMEM)] + [whole] * 7,
        out_shape=(part, part, jax.ShapeDtypeStruct((2, 3, HALF, LANES), f32)),
        scratch_shapes=[
            pltpu.VMEM((2, 2, lines, 4 * LANES), bf16),
            pltpu.VMEM((2, planes, LANES, 3 * LANES), bf16),
            pltpu.VMEM((2, 2, lines, 3 * LANES), bf16),
            pltpu.VMEM((2, 3, HALF, LANES), f32),
            pltpu.VMEM((2, 3, HALF, LANES), f32),
        ],
        compiler_params=params,
        name="normal",
    )(core, moved.reshape(devices * ROWS, LANES), sampling[0], *tables)
    swap = [(i, i ^ 1) for i in range(lax.axis_size("slab"))]
    other = lax.ppermute(send, "slab", swap)
    result = pl.pallas_call(
        finish_kernel,
        out_shape=jax.ShapeDtypeStruct((devices, LANES), f32),
        compiler_params=params,
        name="finish",
    )(own, other, field)
    home = lax.all_to_all(result.reshape(devices, 1, LANES), axes, 0, 0, tiled=True).reshape(devices, LANES)
    out = jax.ShapeDtypeStruct(direction.shape, f32)
    return tuple(
        pl.pallas_call(update_kernel, out_shape=(out, out, out), compiler_params=params, name="update")(
            home, solution, residual, direction
        )
    )


def solution(mesh):
    image = P(None, None, "slab", "coil", None)
    in_specs = (image, image, image, P(None, "coil", "slab", None, None), P())
    return jax.shard_map(body, mesh=mesh, in_specs=in_specs, out_specs=(image, image, image), check_vma=False)
```

```python
import math

import jax
import jax.numpy as jnp
import ml_dtypes
import numpy as np
from jax import lax
from jax.experimental import pallas as pl
from jax.experimental.pallas import tpu as pltpu
from jax.sharding import PartitionSpec as P

damping_weight = 0.5

LANES = 128
ROWS = 8
MESSAGE_D = 6
MESSAGE_R = 7
HALF = 64
SUMS_AT = 48


def split_pair(table):
    high = table.astype(ml_dtypes.bfloat16)
    low = (table - high.astype(np.float64)).astype(ml_dtypes.bfloat16)
    return np.stack([high, low])


def angles(length):
    index = np.arange(length)
    angle = (index[:, None] * index[None, :] % length) * (2.0 * math.pi / length)
    scale = 1.0 / math.sqrt(length)
    return np.cos(angle) * scale, np.sin(angle) * scale


def make_tables(size_x, size_y):
    cos_y, sin_y = angles(size_y)
    cos_x, sin_x = angles(size_x)
    re_from_re = np.concatenate([cos_y[:, :LANES], -sin_y[:, :LANES], cos_y[:, LANES:], -sin_y[:, LANES:]], axis=1)
    re_from_im = np.concatenate([sin_y[:, :LANES], cos_y[:, :LANES], sin_y[:, LANES:], cos_y[:, LANES:]], axis=1)
    fwd_y = np.concatenate([re_from_re[:LANES], re_from_im[:LANES], re_from_re[LANES:], re_from_im[LANES:]], axis=0)
    order = np.concatenate([np.arange(0, size_x, 2), np.arange(1, size_x, 2)])
    fwd_x = np.concatenate([cos_x[:, order], sin_x[:, order]], axis=0)
    inv_x = np.concatenate([cos_x[order], sin_x[order]], axis=0)
    return [split_pair(t) for t in (fwd_y, fwd_y.T, fwd_x, inv_x)]


def pack_kernel(maps_hbm, direction_hbm, residual_hbm, out_ref, maps_ref, direction_ref, residual_ref, maps_sem, image_sem):
    cells = maps_ref.shape[4]
    copies = [
        pltpu.make_async_copy(maps_hbm.at[part, core], maps_ref.at[part, core], maps_sem.at[part, core])
        for core in range(2)
        for part in range(2)
    ]
    images = [
        pltpu.make_async_copy(direction_hbm, direction_ref, image_sem.at[0]),
        pltpu.make_async_copy(residual_hbm, residual_ref, image_sem.at[1]),
    ]
    for copy in images + copies:
        copy.start()

    def put(core, slot, block):
        out_ref[pl.ds(core * ROWS + slot, cells, stride=2 * ROWS), :] = block.T

    for copy in images:
        copy.wait()
    own = direction_ref.shape[3]
    pieces = [direction_ref[part, 0, row] for part in range(2) for row in range(2)]
    filler = jnp.zeros((LANES - 4 * own, cells), jnp.float32)
    field = jnp.concatenate(pieces + [filler], axis=0)
    for core in range(2):
        put(core, MESSAGE_D, field)
        filler = jnp.zeros((LANES - 2 * own, cells), jnp.float32)
        put(core, MESSAGE_R, jnp.concatenate([residual_ref[core, 0, 0], residual_ref[core, 0, 1], filler], axis=0))
    for core in range(2):
        for part in range(2):
            copies[core * 2 + part].wait()
            for row in range(2):
                put(core, part * 2 + row, maps_ref[part, core, row, :LANES, :])
            put(
                core,
                4 + part,
                jnp.concatenate([maps_ref[part, core, 0, LANES:, :], maps_ref[part, core, 1, LANES:, :]], axis=0),
            )


def lane_index(rows):
    return lax.broadcasted_iota(jnp.int32, (rows, LANES), 1)


def spread(blocks, own, slots):
    lane = lane_index(HALF)
    result = []
    for slot in slots:
        low = jnp.zeros((HALF, LANES), jnp.float32)
        high = jnp.zeros((HALF, LANES), jnp.float32)
        for c, block in enumerate(blocks):
            start = c * own
            moved = pltpu.roll(block, (start - slot * own) % LANES, 1)
            if start < LANES:
                low = jnp.where((lane >= start) & (lane < start + own), moved, low)
            if start + own > LANES:
                at = start - LANES
                high = jnp.where((lane >= at) & (lane < at + own), moved, high)
        result.append((low, high))
    return result


def join_low(first, second):
    return jnp.where(lane_index(HALF) < HALF, first, pltpu.roll(second, HALF, 1))


def join_high(first, second):
    return jnp.where(lane_index(HALF) < HALF, pltpu.roll(first, HALF, 1), second)


def halves(value):
    high = value.astype(jnp.bfloat16)
    low = (value - high.astype(jnp.float32)).astype(jnp.bfloat16)
    return high, low


def dot3(left_high, left_low, right_high, right_low):
    def dot(a, b):
        return jnp.dot(a, b, preferred_element_type=jnp.float32)

    return dot(left_high, right_high) + (dot(left_high, right_low) + dot(left_low, right_high))


def normal_kernel(
    core_ref,
    recv_ref,
    weight_ref,
    fwd_y_ref,
    inv_y_ref,
    fwd_x_ref,
    inv_x_ref,
    own_ref,
    send_ref,
    field_ref,
    line_ref,
    mid_ref,
    total_ref,
    image_ref,
):
    coils = recv_ref.shape[0] // (ROWS * HALF)
    own = 2 * 96 // coils

    def load(c, slot):
        return recv_ref[pl.ds(c * HALF * ROWS + slot, HALF, stride=ROWS), :]

    pieces = spread([load(c, MESSAGE_D) for c in range(coils)], own, range(4))
    for part in range(2):
        (low0, high0), (low1, high1) = pieces[2 * part], pieces[2 * part + 1]
        image_ref[part, 0] = low0
        image_ref[part, 1] = low1
        image_ref[part, 2] = join_low(high0, high1)

    def store_line(row, c, column, value):
        for term, half in enumerate(halves(value)):
            line_ref[term, row, c * HALF : (c + 1) * HALF, column * LANES : (column + 1) * LANES] = half

    for c in range(coils):
        for slot in range(3):
            s_re = load(c, slot if slot < 2 else 4)
            s_im = load(c, slot + 2 if slot < 2 else 5)
            d_re, d_im = image_ref[0, slot], image_ref[1, slot]
            x_re = s_re * d_re - s_im * d_im
            x_im = s_re * d_im + s_im * d_re
            if slot < 2:
                store_line(slot, c, 0, x_re)
                store_line(slot, c, 1, x_im)
            else:
                store_line(0, c, 2, join_low(x_re, x_im))
                store_line(1, c, 2, join_high(x_re, x_im))
    for row in range(2):
        spectra = dot3(line_ref[0, row], line_ref[1, row], fwd_y_ref[0], fwd_y_ref[1])
        for term, half in enumerate(halves(spectra)):
            for c in range(coils):
                mid_ref[term, c, row * HALF : (row + 1) * HALF, :] = half[c * HALF : (c + 1) * HALF]
    weight_low = weight_ref[:LANES].astype(jnp.float32).T
    weight_high = weight_ref[LANES:].astype(jnp.float32).T
    weight_mix = jnp.concatenate([weight_high, weight_high], axis=1)
    sign = jnp.where(lane_index(LANES) < HALF, 1.0, -1.0).astype(jnp.float32)
    for c in range(coils):
        both = dot3(fwd_x_ref[0], fwd_x_ref[1], mid_ref[0, c], mid_ref[1, c])
        p, q = both[:LANES], both[LANES:]
        turned = sign * pltpu.roll(q[:, 2 * LANES :], HALF, 1)
        masked = jnp.concatenate(
            [
                (p[:, :LANES] + q[:, LANES : 2 * LANES]) * weight_low,
                (p[:, LANES : 2 * LANES] - q[:, :LANES]) * weight_low,
                (p[:, 2 * LANES :] + turned) * weight_mix,
            ],
            axis=1,
        )
        masked_high, masked_low = halves(masked)
        both = dot3(inv_x_ref[0], inv_x_ref[1], masked_high, masked_low)
        p, q = both[:LANES], both[LANES:]
        turned = sign * pltpu.roll(q[:, 2 * LANES :], HALF, 1)
        columns = (
            p[:, :LANES] - q[:, LANES : 2 * LANES],
            p[:, LANES : 2 * LANES] + q[:, :LANES],
            p[:, 2 * LANES :] - turned,
        )
        for column, value in enumerate(columns):
            for row in range(2):
                store_line(row, c, column, value[row * HALF : (row + 1) * HALF])
    lines = [dot3(line_ref[0, row], line_ref[1, row], inv_y_ref[0], inv_y_ref[1]) for row in range(2)]
    for slot in range(3):
        sum_re = jnp.zeros((HALF, LANES), jnp.float32)
        sum_im = jnp.zeros((HALF, LANES), jnp.float32)
        for c in range(coils):
            rows = slice(c * HALF, (c + 1) * HALF)
            s_re = load(c, slot if slot < 2 else 4)
            s_im = load(c, slot + 2 if slot < 2 else 5)
            if slot < 2:
                y_re, y_im = lines[slot][rows, :LANES], lines[slot][rows, LANES : 2 * LANES]
            else:
                first, second = lines[0][rows, 2 * LANES :], lines[1][rows, 2 * LANES :]
                y_re, y_im = join_low(first, second), join_high(first, second)
            sum_re = sum_re + (s_re * y_re + s_im * y_im)
            sum_im = sum_im + (s_re * y_im - s_im * y_re)
        total_ref[0, slot] = sum_re
        total_ref[1, slot] = sum_im
    core = core_ref[0]
    own_ref[...] = total_ref[core]
    send_ref[...] = total_ref[1 - core]
    field_ref[0] = image_ref[core]
    pieces = spread([load(c, MESSAGE_R) for c in range(coils)], own, range(2))
    field_ref[1, 0] = pieces[0][0]
    field_ref[1, 1] = pieces[1][0]
    field_ref[1, 2] = join_low(pieces[0][1], pieces[1][1])


def finish_kernel(own_ref, other_ref, field_ref, out_ref):
    direction = field_ref[0]
    residual = field_ref[1]
    image_ap = own_ref[...] + other_ref[...] + damping_weight * direction
    lane = lane_index(HALF)
    coils = out_ref.shape[0] // HALF
    own = 2 * 96 // coils
    sums = jnp.zeros((HALF, LANES), jnp.float32)
    products = (residual * residual, direction * image_ap, residual * image_ap, image_ap * image_ap)
    for index, product in enumerate(products):
        sums = jnp.where(lane == SUMS_AT + index, jnp.sum(product), sums)
    high = image_ap[2]
    for c in range(coils):
        start = c * own
        block = sums
        for row in range(2):
            at = row * own
            inside = (lane >= at) & (lane < at + own)
            if start < LANES:
                block = jnp.where(inside, pltpu.roll(image_ap[row], (at - start) % LANES, 1), block)
            if start + own > LANES:
                moved = pltpu.roll(high, (at - (start - LANES + row * HALF)) % LANES, 1)
                if start < LANES:
                    inside = inside & (lane >= at + LANES - start)
                block = jnp.where(inside, moved, block)
        out_ref[c * HALF : (c + 1) * HALF, :] = block


def update_kernel(
    recv_ref, solution_ref, residual_ref, direction_ref, next_solution_ref, next_residual_ref, next_direction_ref
):
    cells = recv_ref.shape[0] // 2
    own = direction_ref.shape[3]
    totals = jnp.sum(recv_ref[...], axis=0, keepdims=True)
    lane = lax.broadcasted_iota(jnp.int32, (1, LANES), 1)

    def pick(index):
        return jnp.sum(jnp.where(lane == SUMS_AT + index, totals, 0.0), axis=1, keepdims=True)

    norm_now, curvature, cross, square = pick(0), pick(1), pick(2), pick(3)
    alpha = norm_now / curvature
    fresh = jnp.maximum(norm_now + alpha * (alpha * square - 2.0 * cross), 0.0)
    beta = fresh / norm_now
    for part in range(2):
        turned = recv_ref[pl.ds(part, cells, stride=2), :].T
        for row in range(2):
            image_ap = turned[row * own : (row + 1) * own]
            direction = direction_ref[part, 0, row]
            next_residual = residual_ref[part, 0, row] - alpha * image_ap
            next_solution_ref[part, 0, row] = solution_ref[part, 0, row] + alpha * direction
            next_residual_ref[part, 0, row] = next_residual
            next_direction_ref[part, 0, row] = next_residual + beta * direction


def normal_scratch(planes):
    return [
        pltpu.VMEM((2, 2, planes * HALF, 3 * LANES), jnp.bfloat16),
        pltpu.VMEM((2, planes, LANES, 3 * LANES), jnp.bfloat16),
        pltpu.VMEM((2, 3, HALF, LANES), jnp.float32),
        pltpu.VMEM((2, 3, HALF, LANES), jnp.float32),
    ]


def body(solution, residual, direction, sens_maps, sampling):
    axes = ("coil", "slab")
    devices = lax.axis_size(axes)
    planes = lax.axis_size("coil")
    f32 = jnp.float32
    params = pltpu.CompilerParams(vmem_limit_bytes=24 * 1024 * 1024)
    hbm = pl.BlockSpec(memory_space=pltpu.HBM)
    whole = pl.BlockSpec(memory_space=pltpu.VMEM)
    packed = pl.pallas_call(
        pack_kernel,
        in_specs=[hbm] * 3,
        out_shape=jax.ShapeDtypeStruct((devices * ROWS, LANES), f32),
        scratch_shapes=[pltpu.VMEM(a.shape, f32) for a in (sens_maps, direction, residual)]
        + [pltpu.SemaphoreType.DMA((2, 2)), pltpu.SemaphoreType.DMA((2,))],
        compiler_params=params,
        name="pack",
    )(sens_maps, direction, residual)
    core = (lax.axis_index("slab") % 2).astype(jnp.int32).reshape(1)
    packed, core = lax.optimization_barrier((packed, core))
    moved = lax.all_to_all(packed.reshape(devices, ROWS, LANES), axes, 0, 0, tiled=True)
    tables = [jnp.asarray(t) for t in make_tables(sampling.shape[1], sampling.shape[2])]
    part = jax.ShapeDtypeStruct((3, HALF, LANES), f32)
    own, send, field = pl.pallas_call(
        normal_kernel,
        in_specs=[pl.BlockSpec(memory_space=pltpu.SMEM)] + [whole] * (2 + len(tables)),
        out_shape=(part, part, jax.ShapeDtypeStruct((2, 3, HALF, LANES), f32)),
        scratch_shapes=normal_scratch(planes),
        compiler_params=params,
        name="normal",
    )(core, moved.reshape(devices * ROWS, LANES), sampling[0].T, *tables)
    swap = [(i, i ^ 1) for i in range(lax.axis_size("slab"))]
    other = lax.ppermute(send, "slab", swap)
    result = pl.pallas_call(
        finish_kernel,
        out_shape=jax.ShapeDtypeStruct((devices, LANES), f32),
        compiler_params=params,
        name="finish",
    )(own, other, field)
    home = lax.all_to_all(result.reshape(devices, 1, LANES), axes, 0, 0, tiled=True).reshape(devices, LANES)
    out = jax.ShapeDtypeStruct(direction.shape, f32)
    return tuple(
        pl.pallas_call(update_kernel, out_shape=(out, out, out), compiler_params=params, name="update")(
            home, solution, residual, direction
        )
    )


def solution(mesh):
    image = P(None, None, "slab", "coil", None)
    in_specs = (image, image, image, P(None, "coil", "slab", None, None), P())
    return jax.shard_map(body, mesh=mesh, in_specs=in_specs, out_specs=(image, image, image), check_vma=False)
```

```python
import math

import jax
import jax.numpy as jnp
import ml_dtypes
import numpy as np
from jax import lax
from jax.experimental import pallas as pl
from jax.experimental.pallas import tpu as pltpu
from jax.sharding import PartitionSpec as P

damping_weight = 0.5

LANES = 128
ROWS = 8
MESSAGE_D = 6
MESSAGE_R = 7
HALF = 64
SUMS_AT = 48


def split_pair(table):
    high = table.astype(ml_dtypes.bfloat16)
    low = (table - high.astype(np.float64)).astype(ml_dtypes.bfloat16)
    return np.stack([high, low])


def angles(length):
    index = np.arange(length)
    angle = (index[:, None] * index[None, :] % length) * (2.0 * math.pi / length)
    scale = 1.0 / math.sqrt(length)
    return np.cos(angle) * scale, np.sin(angle) * scale


def make_tables(size_x, size_y):
    cos_y, sin_y = angles(size_y)
    cos_x, sin_x = angles(size_x)
    re_from_re = np.concatenate([cos_y[:, :LANES], -sin_y[:, :LANES], cos_y[:, LANES:], -sin_y[:, LANES:]], axis=1)
    re_from_im = np.concatenate([sin_y[:, :LANES], cos_y[:, :LANES], sin_y[:, LANES:], cos_y[:, LANES:]], axis=1)
    fwd_y = np.concatenate([re_from_re[:LANES], re_from_im[:LANES], re_from_re[LANES:], re_from_im[LANES:]], axis=0)
    order = np.concatenate([np.arange(0, size_x, 2), np.arange(1, size_x, 2)])
    fwd_x = np.concatenate([cos_x[:, order], sin_x[:, order]], axis=0)
    inv_x = np.concatenate([cos_x[order], sin_x[order]], axis=0)
    return [split_pair(t) for t in (fwd_y, fwd_y.T, fwd_x, inv_x)]


def pack_kernel(maps_hbm, direction_hbm, residual_hbm, out_ref, maps_ref, direction_ref, residual_ref, maps_sem, image_sem):
    cells = maps_ref.shape[4]
    copies = [
        pltpu.make_async_copy(maps_hbm.at[part, core], maps_ref.at[part, core], maps_sem.at[part, core])
        for core in range(2)
        for part in range(2)
    ]
    images = [
        pltpu.make_async_copy(direction_hbm, direction_ref, image_sem.at[0]),
        pltpu.make_async_copy(residual_hbm, residual_ref, image_sem.at[1]),
    ]
    for copy in images + copies:
        copy.start()

    def put(core, slot, block):
        out_ref[pl.ds(core * ROWS + slot, cells, stride=2 * ROWS), :] = block.T

    for copy in images:
        copy.wait()
    own = direction_ref.shape[3]
    pieces = [direction_ref[part, 0, row] for part in range(2) for row in range(2)]
    filler = jnp.zeros((LANES - 4 * own, cells), jnp.float32)
    field = jnp.concatenate(pieces + [filler], axis=0)
    for core in range(2):
        put(core, MESSAGE_D, field)
        filler = jnp.zeros((LANES - 2 * own, cells), jnp.float32)
        put(core, MESSAGE_R, jnp.concatenate([residual_ref[core, 0, 0], residual_ref[core, 0, 1], filler], axis=0))
    for core in range(2):
        for part in range(2):
            copies[core * 2 + part].wait()
            for row in range(2):
                put(core, part * 2 + row, maps_ref[part, core, row, :LANES, :])
            put(
                core,
                4 + part,
                jnp.concatenate([maps_ref[part, core, 0, LANES:, :], maps_ref[part, core, 1, LANES:, :]], axis=0),
            )


def lane_index(rows):
    return lax.broadcasted_iota(jnp.int32, (rows, LANES), 1)


def spread(blocks, own, slots):
    lane = lane_index(HALF)
    result = []
    for slot in slots:
        low = jnp.zeros((HALF, LANES), jnp.float32)
        high = jnp.zeros((HALF, LANES), jnp.float32)
        for c, block in enumerate(blocks):
            start = c * own
            moved = pltpu.roll(block, (start - slot * own) % LANES, 1)
            if start < LANES:
                low = jnp.where((lane >= start) & (lane < start + own), moved, low)
            if start + own > LANES:
                at = start - LANES
                high = jnp.where((lane >= at) & (lane < at + own), moved, high)
        result.append((low, high))
    return result


def join_low(first, second):
    return jnp.where(lane_index(HALF) < HALF, first, pltpu.roll(second, HALF, 1))


def join_high(first, second):
    return jnp.where(lane_index(HALF) < HALF, pltpu.roll(first, HALF, 1), second)


def halves(value):
    high = value.astype(jnp.bfloat16)
    low = (value - high.astype(jnp.float32)).astype(jnp.bfloat16)
    return high, low


def dot3(left_high, left_low, right_high, right_low):
    def dot(a, b):
        return jnp.dot(a, b, preferred_element_type=jnp.float32)

    return dot(left_high, right_high) + (dot(left_high, right_low) + dot(left_low, right_high))


def normal_kernel(
    core_ref,
    recv_ref,
    weight_ref,
    fwd_y_ref,
    inv_y_ref,
    fwd_x_ref,
    inv_x_ref,
    own_ref,
    send_ref,
    field_ref,
    line_ref,
    mid_ref,
    total_ref,
    image_ref,
):
    coils = recv_ref.shape[0] // (ROWS * HALF)
    own = 2 * 96 // coils

    def load(c, slot):
        return recv_ref[pl.ds(c * HALF * ROWS + slot, HALF, stride=ROWS), :]

    pieces = spread([load(c, MESSAGE_D) for c in range(coils)], own, range(4))
    for part in range(2):
        (low0, high0), (low1, high1) = pieces[2 * part], pieces[2 * part + 1]
        image_ref[part, 0] = low0
        image_ref[part, 1] = low1
        image_ref[part, 2] = join_low(high0, high1)

    def store_line(row, c, column, value):
        for term, half in enumerate(halves(value)):
            line_ref[term, row, c * HALF : (c + 1) * HALF, column * LANES : (column + 1) * LANES] = half

    for c in range(coils):
        for slot in range(3):
            s_re = load(c, slot if slot < 2 else 4)
            s_im = load(c, slot + 2 if slot < 2 else 5)
            d_re, d_im = image_ref[0, slot], image_ref[1, slot]
            x_re = s_re * d_re - s_im * d_im
            x_im = s_re * d_im + s_im * d_re
            if slot < 2:
                store_line(slot, c, 0, x_re)
                store_line(slot, c, 1, x_im)
            else:
                store_line(0, c, 2, join_low(x_re, x_im))
                store_line(1, c, 2, join_high(x_re, x_im))
    for row in range(2):
        spectra = dot3(line_ref[0, row], line_ref[1, row], fwd_y_ref[0], fwd_y_ref[1])
        for term, half in enumerate(halves(spectra)):
            for c in range(coils):
                mid_ref[term, c, row * HALF : (row + 1) * HALF, :] = half[c * HALF : (c + 1) * HALF]
    weight_low = weight_ref[:LANES].astype(jnp.float32).T
    weight_high = weight_ref[LANES:].astype(jnp.float32).T
    weight_mix = jnp.concatenate([weight_high, weight_high], axis=1)
    sign = jnp.where(lane_index(LANES) < HALF, 1.0, -1.0).astype(jnp.float32)
    for c in range(coils):
        both = dot3(fwd_x_ref[0], fwd_x_ref[1], mid_ref[0, c], mid_ref[1, c])
        p, q = both[:LANES], both[LANES:]
        turned = sign * pltpu.roll(q[:, 2 * LANES :], HALF, 1)
        masked = jnp.concatenate(
            [
                (p[:, :LANES] + q[:, LANES : 2 * LANES]) * weight_low,
                (p[:, LANES : 2 * LANES] - q[:, :LANES]) * weight_low,
                (p[:, 2 * LANES :] + turned) * weight_mix,
            ],
            axis=1,
        )
        masked_high, masked_low = halves(masked)
        both = dot3(inv_x_ref[0], inv_x_ref[1], masked_high, masked_low)
        p, q = both[:LANES], both[LANES:]
        turned = sign * pltpu.roll(q[:, 2 * LANES :], HALF, 1)
        columns = (
            p[:, :LANES] - q[:, LANES : 2 * LANES],
            p[:, LANES : 2 * LANES] + q[:, :LANES],
            p[:, 2 * LANES :] - turned,
        )
        for column, value in enumerate(columns):
            for row in range(2):
                store_line(row, c, column, value[row * HALF : (row + 1) * HALF])
    lines = [dot3(line_ref[0, row], line_ref[1, row], inv_y_ref[0], inv_y_ref[1]) for row in range(2)]
    for slot in range(3):
        sum_re = jnp.zeros((HALF, LANES), jnp.float32)
        sum_im = jnp.zeros((HALF, LANES), jnp.float32)
        for c in range(coils):
            rows = slice(c * HALF, (c + 1) * HALF)
            s_re = load(c, slot if slot < 2 else 4)
            s_im = load(c, slot + 2 if slot < 2 else 5)
            if slot < 2:
                y_re, y_im = lines[slot][rows, :LANES], lines[slot][rows, LANES : 2 * LANES]
            else:
                first, second = lines[0][rows, 2 * LANES :], lines[1][rows, 2 * LANES :]
                y_re, y_im = join_low(first, second), join_high(first, second)
            sum_re = sum_re + (s_re * y_re + s_im * y_im)
            sum_im = sum_im + (s_re * y_im - s_im * y_re)
        total_ref[0, slot] = sum_re
        total_ref[1, slot] = sum_im
    core = core_ref[0]
    own_ref[...] = total_ref[core]
    send_ref[...] = total_ref[1 - core]
    field_ref[0] = image_ref[core]
    pieces = spread([load(c, MESSAGE_R) for c in range(coils)], own, range(2))
    field_ref[1, 0] = pieces[0][0]
    field_ref[1, 1] = pieces[1][0]
    field_ref[1, 2] = join_low(pieces[0][1], pieces[1][1])


def finish_kernel(own_ref, other_ref, field_ref, out_ref):
    direction = field_ref[0]
    residual = field_ref[1]
    image_ap = own_ref[...] + other_ref[...] + damping_weight * direction
    lane = lane_index(HALF)
    coils = out_ref.shape[0] // HALF
    own = 2 * 96 // coils
    sums = jnp.zeros((HALF, LANES), jnp.float32)
    products = (residual * residual, direction * image_ap, residual * image_ap, image_ap * image_ap)
    for index, product in enumerate(products):
        sums = jnp.where(lane == SUMS_AT + index, jnp.sum(product), sums)
    high = image_ap[2]
    for c in range(coils):
        start = c * own
        block = sums
        for row in range(2):
            at = row * own
            inside = (lane >= at) & (lane < at + own)
            if start < LANES:
                block = jnp.where(inside, pltpu.roll(image_ap[row], (at - start) % LANES, 1), block)
            if start + own > LANES:
                moved = pltpu.roll(high, (at - (start - LANES + row * HALF)) % LANES, 1)
                if start < LANES:
                    inside = inside & (lane >= at + LANES - start)
                block = jnp.where(inside, moved, block)
        out_ref[c * HALF : (c + 1) * HALF, :] = block


def update_kernel(
    recv_ref, solution_ref, residual_ref, direction_ref, next_solution_ref, next_residual_ref, next_direction_ref
):
    cells = recv_ref.shape[0] // 2
    own = direction_ref.shape[3]
    totals = jnp.sum(recv_ref[...], axis=0, keepdims=True)
    lane = lax.broadcasted_iota(jnp.int32, (1, LANES), 1)

    def pick(index):
        return jnp.sum(jnp.where(lane == SUMS_AT + index, totals, 0.0), axis=1, keepdims=True)

    norm_now, curvature, cross, square = pick(0), pick(1), pick(2), pick(3)
    alpha = norm_now / curvature
    fresh = jnp.maximum(norm_now + alpha * (alpha * square - 2.0 * cross), 0.0)
    beta = fresh / norm_now
    for part in range(2):
        turned = recv_ref[pl.ds(part, cells, stride=2), :].T
        for row in range(2):
            image_ap = turned[row * own : (row + 1) * own]
            direction = direction_ref[part, 0, row]
            next_residual = residual_ref[part, 0, row] - alpha * image_ap
            next_solution_ref[part, 0, row] = solution_ref[part, 0, row] + alpha * direction
            next_residual_ref[part, 0, row] = next_residual
            next_direction_ref[part, 0, row] = next_residual + beta * direction


def normal_scratch(planes):
    return [
        pltpu.VMEM((2, 2, planes * HALF, 3 * LANES), jnp.bfloat16),
        pltpu.VMEM((2, planes, LANES, 3 * LANES), jnp.bfloat16),
        pltpu.VMEM((2, 3, HALF, LANES), jnp.float32),
        pltpu.VMEM((2, 3, HALF, LANES), jnp.float32),
    ]


def body(solution, residual, direction, sens_maps, sampling):
    axes = ("coil", "slab")
    devices = lax.axis_size(axes)
    planes = lax.axis_size("coil")
    f32 = jnp.float32
    params = pltpu.CompilerParams(vmem_limit_bytes=24 * 1024 * 1024)
    hbm = pl.BlockSpec(memory_space=pl.ANY)
    whole = pl.BlockSpec(memory_space=pltpu.VMEM)
    packed = pl.pallas_call(
        pack_kernel,
        in_specs=[hbm] * 3,
        out_shape=jax.ShapeDtypeStruct((devices * ROWS, LANES), f32),
        scratch_shapes=[pltpu.VMEM(a.shape, f32) for a in (sens_maps, direction, residual)]
        + [pltpu.SemaphoreType.DMA((2, 2)), pltpu.SemaphoreType.DMA((2,))],
        compiler_params=params,
        name="pack",
    )(*(pltpu.with_memory_space_constraint(a, pltpu.HBM) for a in (sens_maps, direction, residual)))
    core = (lax.axis_index("slab") % 2).astype(jnp.int32).reshape(1)
    packed, core = lax.optimization_barrier((packed, core))
    moved = lax.all_to_all(packed.reshape(devices, ROWS, LANES), axes, 0, 0, tiled=True)
    tables = [jnp.asarray(t) for t in make_tables(sampling.shape[1], sampling.shape[2])]
    part = jax.ShapeDtypeStruct((3, HALF, LANES), f32)
    own, send, field = pl.pallas_call(
        normal_kernel,
        in_specs=[pl.BlockSpec(memory_space=pltpu.SMEM)] + [whole] * (2 + len(tables)),
        out_shape=(part, part, jax.ShapeDtypeStruct((2, 3, HALF, LANES), f32)),
        scratch_shapes=normal_scratch(planes),
        compiler_params=params,
        name="normal",
    )(core, moved.reshape(devices * ROWS, LANES), sampling[0].T, *tables)
    swap = [(i, i ^ 1) for i in range(lax.axis_size("slab"))]
    other = lax.ppermute(send, "slab", swap)
    result = pl.pallas_call(
        finish_kernel,
        out_shape=jax.ShapeDtypeStruct((devices, LANES), f32),
        compiler_params=params,
        name="finish",
    )(own, other, field)
    home = lax.all_to_all(result.reshape(devices, 1, LANES), axes, 0, 0, tiled=True).reshape(devices, LANES)
    out = jax.ShapeDtypeStruct(direction.shape, f32)
    return tuple(
        pl.pallas_call(update_kernel, out_shape=(out, out, out), compiler_params=params, name="update")(
            home, solution, residual, direction
        )
    )


def solution(mesh):
    image = P(None, None, "slab", "coil", None)
    in_specs = (image, image, image, P(None, "coil", "slab", None, None), P())
    return jax.shard_map(body, mesh=mesh, in_specs=in_specs, out_specs=(image, image, image), check_vma=False)
```

```python
import math

import jax
import jax.numpy as jnp
import ml_dtypes
import numpy as np
from jax import lax
from jax.experimental import pallas as pl
from jax.experimental.pallas import tpu as pltpu
from jax.sharding import PartitionSpec as P

damping_weight = 0.5

LANES = 128
ROWS = 7
MESSAGE_IMAGE = 6
HALF = 64
SUMS_AT = 48


def split_pair(table):
    high = table.astype(ml_dtypes.bfloat16)
    low = (table - high.astype(np.float64)).astype(ml_dtypes.bfloat16)
    return np.stack([high, low])


def angles(length):
    index = np.arange(length)
    angle = (index[:, None] * index[None, :] % length) * (2.0 * math.pi / length)
    scale = 1.0 / math.sqrt(length)
    return np.cos(angle) * scale, np.sin(angle) * scale


def make_tables(size_x, size_y):
    cos_y, sin_y = angles(size_y)
    cos_x, sin_x = angles(size_x)
    re_from_re = np.concatenate([cos_y[:, :LANES], -sin_y[:, :LANES], cos_y[:, LANES:], -sin_y[:, LANES:]], axis=1)
    re_from_im = np.concatenate([sin_y[:, :LANES], cos_y[:, :LANES], sin_y[:, LANES:], cos_y[:, LANES:]], axis=1)
    fwd_y = np.concatenate([re_from_re[:LANES], re_from_im[:LANES], re_from_re[LANES:], re_from_im[LANES:]], axis=0)
    order = np.concatenate([np.arange(0, size_x, 2), np.arange(1, size_x, 2)])
    fwd_x = np.concatenate([cos_x[:, order], sin_x[:, order]], axis=0)
    inv_x = np.concatenate([cos_x[order], sin_x[order]], axis=0)
    return [split_pair(t) for t in (fwd_y, fwd_y.T, fwd_x, inv_x)]


def pack_kernel(maps_hbm, direction_hbm, residual_hbm, out_ref, maps_ref, direction_ref, residual_ref, maps_sem, image_sem):
    cells = maps_ref.shape[4]
    copies = [
        pltpu.make_async_copy(maps_hbm.at[part, core], maps_ref.at[part, core], maps_sem.at[part, core])
        for core in range(2)
        for part in range(2)
    ]
    images = [
        pltpu.make_async_copy(direction_hbm, direction_ref, image_sem.at[0]),
        pltpu.make_async_copy(residual_hbm, residual_ref, image_sem.at[1]),
    ]
    for copy in images + copies:
        copy.start()

    def put(core, slot, block):
        out_ref[pl.ds(core * ROWS + slot, cells, stride=2 * ROWS), :] = block.T

    for copy in images:
        copy.wait()
    own = direction_ref.shape[3]
    filler = jnp.zeros((LANES - 4 * own, cells), jnp.float32)
    for core in range(2):
        pieces = [image_ref[core, 0, row] for image_ref in (direction_ref, residual_ref) for row in range(2)]
        put(core, MESSAGE_IMAGE, jnp.concatenate(pieces + [filler], axis=0))
    for core in range(2):
        for part in range(2):
            copies[core * 2 + part].wait()
            for row in range(2):
                put(core, part * 2 + row, maps_ref[part, core, row, :LANES, :])
            put(
                core,
                4 + part,
                jnp.concatenate([maps_ref[part, core, 0, LANES:, :], maps_ref[part, core, 1, LANES:, :]], axis=0),
            )


def lane_index(rows):
    return lax.broadcasted_iota(jnp.int32, (rows, LANES), 1)


def spread(blocks, own, slots):
    lane = lane_index(HALF)
    result = []
    for slot in slots:
        low = jnp.zeros((HALF, LANES), jnp.float32)
        high = jnp.zeros((HALF, LANES), jnp.float32)
        for c, block in enumerate(blocks):
            start = c * own
            moved = pltpu.roll(block, (start - slot * own) % LANES, 1)
            if start < LANES:
                low = jnp.where((lane >= start) & (lane < start + own), moved, low)
            if start + own > LANES:
                at = start - LANES
                high = jnp.where((lane >= at) & (lane < at + own), moved, high)
        result.append((low, high))
    return result


def join_low(first, second):
    return jnp.where(lane_index(HALF) < HALF, first, pltpu.roll(second, HALF, 1))


def join_high(first, second):
    return jnp.where(lane_index(HALF) < HALF, pltpu.roll(first, HALF, 1), second)


def halves(value):
    high = value.astype(jnp.bfloat16)
    low = (value - high.astype(jnp.float32)).astype(jnp.bfloat16)
    return high, low


def dot3(left_high, left_low, right_high, right_low):
    def dot(a, b):
        return jnp.dot(a, b, preferred_element_type=jnp.float32)

    return dot(left_high, right_high) + (dot(left_high, right_low) + dot(left_low, right_high))


def load_rows(recv_ref, c, slot):
    return recv_ref[pl.ds(c * HALF * ROWS + slot, HALF, stride=ROWS), :]


def image_kernel(recv_ref, direction_ref, residual_ref):
    coils = recv_ref.shape[0] // (ROWS * HALF)
    own = 2 * 96 // coils
    pieces = spread([load_rows(recv_ref, c, MESSAGE_IMAGE) for c in range(coils)], own, range(4))
    for index, image_ref in enumerate((direction_ref, residual_ref)):
        (low0, high0), (low1, high1) = pieces[2 * index], pieces[2 * index + 1]
        image_ref[0] = low0
        image_ref[1] = low1
        image_ref[2] = join_low(high0, high1)


def normal_kernel(
    core_ref,
    recv_ref,
    own_image_ref,
    other_image_ref,
    weight_ref,
    fwd_y_ref,
    inv_y_ref,
    fwd_x_ref,
    inv_x_ref,
    own_ref,
    send_ref,
    line_ref,
    mid_ref,
    total_ref,
    image_ref,
):
    coils = recv_ref.shape[0] // (ROWS * HALF)
    core = core_ref[0]

    def load(c, slot):
        return load_rows(recv_ref, c, slot)

    image_ref[core] = own_image_ref[...]
    image_ref[1 - core] = other_image_ref[...]

    def store_line(row, c, column, value):
        for term, half in enumerate(halves(value)):
            line_ref[term, row, c * HALF : (c + 1) * HALF, column * LANES : (column + 1) * LANES] = half

    for c in range(coils):
        for slot in range(3):
            s_re = load(c, slot if slot < 2 else 4)
            s_im = load(c, slot + 2 if slot < 2 else 5)
            d_re, d_im = image_ref[0, slot], image_ref[1, slot]
            x_re = s_re * d_re - s_im * d_im
            x_im = s_re * d_im + s_im * d_re
            if slot < 2:
                store_line(slot, c, 0, x_re)
                store_line(slot, c, 1, x_im)
            else:
                store_line(0, c, 2, join_low(x_re, x_im))
                store_line(1, c, 2, join_high(x_re, x_im))
    for row in range(2):
        spectra = dot3(line_ref[0, row], line_ref[1, row], fwd_y_ref[0], fwd_y_ref[1])
        for term, half in enumerate(halves(spectra)):
            for c in range(coils):
                mid_ref[term, c, row * HALF : (row + 1) * HALF, :] = half[c * HALF : (c + 1) * HALF]
    weight_low = weight_ref[:LANES].astype(jnp.float32).T
    weight_high = weight_ref[LANES:].astype(jnp.float32).T
    weight_mix = jnp.concatenate([weight_high, weight_high], axis=1)
    sign = jnp.where(lane_index(LANES) < HALF, 1.0, -1.0).astype(jnp.float32)
    for c in range(coils):
        both = dot3(fwd_x_ref[0], fwd_x_ref[1], mid_ref[0, c], mid_ref[1, c])
        p, q = both[:LANES], both[LANES:]
        turned = sign * pltpu.roll(q[:, 2 * LANES :], HALF, 1)
        masked = jnp.concatenate(
            [
                (p[:, :LANES] + q[:, LANES : 2 * LANES]) * weight_low,
                (p[:, LANES : 2 * LANES] - q[:, :LANES]) * weight_low,
                (p[:, 2 * LANES :] + turned) * weight_mix,
            ],
            axis=1,
        )
        masked_high, masked_low = halves(masked)
        both = dot3(inv_x_ref[0], inv_x_ref[1], masked_high, masked_low)
        p, q = both[:LANES], both[LANES:]
        turned = sign * pltpu.roll(q[:, 2 * LANES :], HALF, 1)
        columns = (
            p[:, :LANES] - q[:, LANES : 2 * LANES],
            p[:, LANES : 2 * LANES] + q[:, :LANES],
            p[:, 2 * LANES :] - turned,
        )
        for column, value in enumerate(columns):
            for row in range(2):
                store_line(row, c, column, value[row * HALF : (row + 1) * HALF])
    lines = [dot3(line_ref[0, row], line_ref[1, row], inv_y_ref[0], inv_y_ref[1]) for row in range(2)]
    for slot in range(3):
        sum_re = jnp.zeros((HALF, LANES), jnp.float32)
        sum_im = jnp.zeros((HALF, LANES), jnp.float32)
        for c in range(coils):
            rows = slice(c * HALF, (c + 1) * HALF)
            s_re = load(c, slot if slot < 2 else 4)
            s_im = load(c, slot + 2 if slot < 2 else 5)
            if slot < 2:
                y_re, y_im = lines[slot][rows, :LANES], lines[slot][rows, LANES : 2 * LANES]
            else:
                first, second = lines[0][rows, 2 * LANES :], lines[1][rows, 2 * LANES :]
                y_re, y_im = join_low(first, second), join_high(first, second)
            sum_re = sum_re + (s_re * y_re + s_im * y_im)
            sum_im = sum_im + (s_re * y_im - s_im * y_re)
        total_ref[0, slot] = sum_re
        total_ref[1, slot] = sum_im
    own_ref[...] = total_ref[core]
    send_ref[...] = total_ref[1 - core]


def finish_kernel(own_ref, other_ref, direction_ref, residual_ref, out_ref):
    direction = direction_ref[...]
    residual = residual_ref[...]
    image_ap = own_ref[...] + other_ref[...] + damping_weight * direction
    lane = lane_index(HALF)
    coils = out_ref.shape[0] // HALF
    own = 2 * 96 // coils
    sums = jnp.zeros((HALF, LANES), jnp.float32)
    products = (residual * residual, direction * image_ap, residual * image_ap, image_ap * image_ap)
    for index, product in enumerate(products):
        sums = jnp.where(lane == SUMS_AT + index, jnp.sum(product), sums)
    high = image_ap[2]
    for c in range(coils):
        start = c * own
        block = sums
        for row in range(2):
            at = row * own
            inside = (lane >= at) & (lane < at + own)
            if start < LANES:
                block = jnp.where(inside, pltpu.roll(image_ap[row], (at - start) % LANES, 1), block)
            if start + own > LANES:
                moved = pltpu.roll(high, (at - (start - LANES + row * HALF)) % LANES, 1)
                if start < LANES:
                    inside = inside & (lane >= at + LANES - start)
                block = jnp.where(inside, moved, block)
        out_ref[c * HALF : (c + 1) * HALF, :] = block


def update_kernel(
    recv_ref, solution_ref, residual_ref, direction_ref, next_solution_ref, next_residual_ref, next_direction_ref
):
    cells = recv_ref.shape[0] // 2
    own = direction_ref.shape[3]
    totals = jnp.sum(recv_ref[...], axis=0, keepdims=True)
    lane = lax.broadcasted_iota(jnp.int32, (1, LANES), 1)

    def pick(index):
        return jnp.sum(jnp.where(lane == SUMS_AT + index, totals, 0.0), axis=1, keepdims=True)

    norm_now, curvature, cross, square = pick(0), pick(1), pick(2), pick(3)
    alpha = norm_now / curvature
    fresh = jnp.maximum(norm_now + alpha * (alpha * square - 2.0 * cross), 0.0)
    beta = fresh / norm_now
    for part in range(2):
        turned = recv_ref[pl.ds(part, cells, stride=2), :].T
        for row in range(2):
            image_ap = turned[row * own : (row + 1) * own]
            direction = direction_ref[part, 0, row]
            next_residual = residual_ref[part, 0, row] - alpha * image_ap
            next_solution_ref[part, 0, row] = solution_ref[part, 0, row] + alpha * direction
            next_residual_ref[part, 0, row] = next_residual
            next_direction_ref[part, 0, row] = next_residual + beta * direction


def normal_scratch(planes):
    return [
        pltpu.VMEM((2, 2, planes * HALF, 3 * LANES), jnp.bfloat16),
        pltpu.VMEM((2, planes, LANES, 3 * LANES), jnp.bfloat16),
        pltpu.VMEM((2, 3, HALF, LANES), jnp.float32),
        pltpu.VMEM((2, 3, HALF, LANES), jnp.float32),
    ]


def body(solution, residual, direction, sens_maps, sampling):
    axes = ("coil", "slab")
    devices = lax.axis_size(axes)
    planes = lax.axis_size("coil")
    f32 = jnp.float32
    params = pltpu.CompilerParams(vmem_limit_bytes=24 * 1024 * 1024)
    hbm = pl.BlockSpec(memory_space=pl.ANY)
    whole = pl.BlockSpec(memory_space=pltpu.VMEM)
    packed = pl.pallas_call(
        pack_kernel,
        in_specs=[hbm] * 3,
        out_shape=jax.ShapeDtypeStruct((devices * ROWS, LANES), f32),
        scratch_shapes=[pltpu.VMEM(a.shape, f32) for a in (sens_maps, direction, residual)]
        + [pltpu.SemaphoreType.DMA((2, 2)), pltpu.SemaphoreType.DMA((2,))],
        compiler_params=params,
        name="pack",
    )(*(pltpu.with_memory_space_constraint(a, pltpu.HBM) for a in (sens_maps, direction, residual)))
    core = (lax.axis_index("slab") % 2).astype(jnp.int32).reshape(1)
    packed, core = lax.optimization_barrier((packed, core))
    moved = lax.all_to_all(packed.reshape(devices * ROWS, 1, LANES), axes, 0, 0, tiled=True)
    moved = moved.reshape(devices * ROWS, LANES)
    tables = [jnp.asarray(t) for t in make_tables(sampling.shape[1], sampling.shape[2])]
    swap = [(i, i ^ 1) for i in range(lax.axis_size("slab"))]
    part = jax.ShapeDtypeStruct((3, HALF, LANES), f32)
    image, residual_image = pl.pallas_call(
        image_kernel, out_shape=(part, part), compiler_params=params, name="image"
    )(moved)
    other_image = lax.ppermute(image, "slab", swap)
    own, send = pl.pallas_call(
        normal_kernel,
        in_specs=[pl.BlockSpec(memory_space=pltpu.SMEM)] + [whole] * (4 + len(tables)),
        out_shape=(part, part),
        scratch_shapes=normal_scratch(planes),
        compiler_params=params,
        name="normal",
    )(core, moved, image, other_image, sampling[0].T, *tables)
    other = lax.ppermute(send, "slab", swap)
    result = pl.pallas_call(
        finish_kernel,
        out_shape=jax.ShapeDtypeStruct((devices, LANES), f32),
        compiler_params=params,
        name="finish",
    )(own, other, image, residual_image)
    home = lax.all_to_all(result.reshape(devices, 1, LANES), axes, 0, 0, tiled=True).reshape(devices, LANES)
    out = jax.ShapeDtypeStruct(direction.shape, f32)
    return tuple(
        pl.pallas_call(update_kernel, out_shape=(out, out, out), compiler_params=params, name="update")(
            home, solution, residual, direction
        )
    )


def solution(mesh):
    image = P(None, None, "slab", "coil", None)
    in_specs = (image, image, image, P(None, "coil", "slab", None, None), P())
    return jax.shard_map(body, mesh=mesh, in_specs=in_specs, out_specs=(image, image, image), check_vma=False)
```

```python
import math

import jax
import jax.numpy as jnp
import ml_dtypes
import numpy as np
from jax import lax
from jax.experimental import pallas as pl
from jax.experimental.pallas import tpu as pltpu
from jax.sharding import Mesh
from jax.sharding import PartitionSpec as P

damping_weight = 0.5

LANES = 128
ROWS = 7
MESSAGE_IMAGE = 6
HALF = 64
QUARTER = 32
SUMS_AT = 96


def split_pair(table):
    high = table.astype(ml_dtypes.bfloat16)
    low = (table - high.astype(np.float64)).astype(ml_dtypes.bfloat16)
    return np.stack([high, low])


def angles(length):
    index = np.arange(length)
    angle = (index[:, None] * index[None, :] % length) * (2.0 * math.pi / length)
    scale = 1.0 / math.sqrt(length)
    return np.cos(angle) * scale, np.sin(angle) * scale


def make_tables(size_x, size_y):
    cos_y, sin_y = angles(size_y)
    cos_x, sin_x = angles(size_x)
    re_from_re = np.concatenate([cos_y[:, :LANES], -sin_y[:, :LANES], cos_y[:, LANES:], -sin_y[:, LANES:]], axis=1)
    re_from_im = np.concatenate([sin_y[:, :LANES], cos_y[:, :LANES], sin_y[:, LANES:], cos_y[:, LANES:]], axis=1)
    fwd_y = np.concatenate([re_from_re[:LANES], re_from_im[:LANES], re_from_re[LANES:], re_from_im[LANES:]], axis=0)
    order = np.arange(size_x).reshape(-1, 2, 2).transpose(2, 1, 0).reshape(-1)
    fwd_x = np.concatenate([cos_x[:, order], sin_x[:, order]], axis=0)
    inv_x = np.concatenate([cos_x[order], sin_x[order]], axis=0)
    return [split_pair(t) for t in (fwd_y, fwd_y.T, fwd_x, inv_x)]


def pack_kernel(maps_hbm, direction_hbm, residual_hbm, out_ref, maps_ref, direction_ref, residual_ref, maps_sem, image_sem):
    cells = maps_ref.shape[4]
    copies = [
        pltpu.make_async_copy(maps_hbm.at[part, core], maps_ref.at[part, core], maps_sem.at[part, core])
        for core in range(2)
        for part in range(2)
    ]
    images = [
        pltpu.make_async_copy(direction_hbm, direction_ref, image_sem.at[0]),
        pltpu.make_async_copy(residual_hbm, residual_ref, image_sem.at[1]),
    ]
    for copy in images + copies:
        copy.start()

    def put(core, slot, block):
        turned = block.T
        for plane in range(cells // QUARTER):
            rows = pl.ds((plane * HALF + core * QUARTER) * ROWS + slot, QUARTER, stride=ROWS)
            out_ref[rows, :] = turned[plane * QUARTER : (plane + 1) * QUARTER]

    for copy in images:
        copy.wait()
    own = direction_ref.shape[3]
    filler = jnp.zeros((LANES - 4 * own, cells), jnp.float32)
    for core in range(2):
        pieces = [image_ref[core, 0, row] for image_ref in (direction_ref, residual_ref) for row in range(2)]
        put(core, MESSAGE_IMAGE, jnp.concatenate(pieces + [filler], axis=0))
    for core in range(2):
        for part in range(2):
            copies[core * 2 + part].wait()
            for row in range(2):
                put(core, part * 2 + row, maps_ref[part, core, row, :LANES, :])
            put(
                core,
                4 + part,
                jnp.concatenate([maps_ref[part, core, 0, LANES:, :], maps_ref[part, core, 1, LANES:, :]], axis=0),
            )


def lane_index(rows):
    return lax.broadcasted_iota(jnp.int32, (rows, LANES), 1)


def spread(blocks, own, slots):
    lane = lane_index(HALF)
    result = []
    for slot in slots:
        low = jnp.zeros((HALF, LANES), jnp.float32)
        high = jnp.zeros((HALF, LANES), jnp.float32)
        for c, block in enumerate(blocks):
            start = c * own
            moved = pltpu.roll(block, (start - slot * own) % LANES, 1)
            if start < LANES:
                low = jnp.where((lane >= start) & (lane < start + own), moved, low)
            if start + own > LANES:
                at = start - LANES
                high = jnp.where((lane >= at) & (lane < at + own), moved, high)
        result.append((low, high))
    return result


def join_low(first, second):
    return jnp.where(lane_index(HALF) < HALF, first, pltpu.roll(second, HALF, 1))


def join_high(first, second):
    return jnp.where(lane_index(HALF) < HALF, pltpu.roll(first, HALF, 1), second)


def halves(value):
    high = value.astype(jnp.bfloat16)
    low = (value - high.astype(jnp.float32)).astype(jnp.bfloat16)
    return high, low


def dot3(left_high, left_low, right_high, right_low):
    def dot(a, b):
        return jnp.dot(a, b, preferred_element_type=jnp.float32)

    return dot(left_high, right_high) + (dot(left_high, right_low) + dot(left_low, right_high))


def load_rows(recv_ref, c, slot):
    return recv_ref[pl.ds(c * HALF * ROWS + slot, HALF, stride=ROWS), :]


def image_kernel(recv_ref, image_ref):
    coils = recv_ref.shape[0] // (ROWS * HALF)
    own = 2 * 96 // coils
    pieces = spread([load_rows(recv_ref, c, MESSAGE_IMAGE) for c in range(coils)], own, range(4))
    for index in range(2):
        (low0, high0), (low1, high1) = pieces[2 * index], pieces[2 * index + 1]
        image_ref[index, 0] = low0
        image_ref[index, 1] = low1
        image_ref[index, 2] = join_low(high0, high1)


def normal_kernel(
    core_ref,
    recv_ref,
    own_image_ref,
    other_image_ref,
    weight_ref,
    fwd_y_ref,
    inv_y_ref,
    fwd_x_ref,
    inv_x_ref,
    total_ref,
    line_ref,
    mid_ref,
    image_ref,
):
    coils = recv_ref.shape[0] // (ROWS * HALF)
    core = core_ref[0]

    def load(c, slot):
        return load_rows(recv_ref, c, slot)

    image_ref[core] = own_image_ref[0]
    image_ref[1 - core] = other_image_ref[0]

    def store_line(row, c, column, value):
        for term, half in enumerate(halves(value)):
            line_ref[term, row, c * HALF : (c + 1) * HALF, column * LANES : (column + 1) * LANES] = half

    for c in range(coils):
        for slot in range(3):
            s_re = load(c, slot if slot < 2 else 4)
            s_im = load(c, slot + 2 if slot < 2 else 5)
            d_re, d_im = image_ref[0, slot], image_ref[1, slot]
            x_re = s_re * d_re - s_im * d_im
            x_im = s_re * d_im + s_im * d_re
            if slot < 2:
                store_line(slot, c, 0, x_re)
                store_line(slot, c, 1, x_im)
            else:
                store_line(0, c, 2, join_low(x_re, x_im))
                store_line(1, c, 2, join_high(x_re, x_im))
    for row in range(2):
        spectra = dot3(line_ref[0, row], line_ref[1, row], fwd_y_ref[0], fwd_y_ref[1])
        for term, half in enumerate(halves(spectra)):
            for c in range(coils):
                mid_ref[term, c, row * HALF : (row + 1) * HALF, :] = half[c * HALF : (c + 1) * HALF]
    weight_low = weight_ref[:LANES].astype(jnp.float32).T
    weight_high = weight_ref[LANES:].astype(jnp.float32).T
    weight_mix = jnp.concatenate([weight_high, weight_high], axis=1)
    sign = jnp.where(lane_index(LANES) < HALF, 1.0, -1.0).astype(jnp.float32)
    for c in range(coils):
        both = dot3(fwd_x_ref[0], fwd_x_ref[1], mid_ref[0, c], mid_ref[1, c])
        p, q = both[:LANES], both[LANES:]
        turned = sign * pltpu.roll(q[:, 2 * LANES :], HALF, 1)
        masked = jnp.concatenate(
            [
                (p[:, :LANES] + q[:, LANES : 2 * LANES]) * weight_low,
                (p[:, LANES : 2 * LANES] - q[:, :LANES]) * weight_low,
                (p[:, 2 * LANES :] + turned) * weight_mix,
            ],
            axis=1,
        )
        masked_high, masked_low = halves(masked)
        both = dot3(inv_x_ref[0], inv_x_ref[1], masked_high, masked_low)
        p, q = both[:LANES], both[LANES:]
        turned = sign * pltpu.roll(q[:, 2 * LANES :], HALF, 1)
        columns = (
            p[:, :LANES] - q[:, LANES : 2 * LANES],
            p[:, LANES : 2 * LANES] + q[:, :LANES],
            p[:, 2 * LANES :] - turned,
        )
        for column, value in enumerate(columns):
            for row in range(2):
                store_line(row, c, column, value[row * HALF : (row + 1) * HALF])
    lines = [dot3(line_ref[0, row], line_ref[1, row], inv_y_ref[0], inv_y_ref[1]) for row in range(2)]
    for slot in range(3):
        sum_re = jnp.zeros((HALF, LANES), jnp.float32)
        sum_im = jnp.zeros((HALF, LANES), jnp.float32)
        for c in range(coils):
            rows = slice(c * HALF, (c + 1) * HALF)
            s_re = load(c, slot if slot < 2 else 4)
            s_im = load(c, slot + 2 if slot < 2 else 5)
            if slot < 2:
                y_re, y_im = lines[slot][rows, :LANES], lines[slot][rows, LANES : 2 * LANES]
            else:
                first, second = lines[0][rows, 2 * LANES :], lines[1][rows, 2 * LANES :]
                y_re, y_im = join_low(first, second), join_high(first, second)
            sum_re = sum_re + (s_re * y_re + s_im * y_im)
            sum_im = sum_im + (s_re * y_im - s_im * y_re)
        total_ref[0, slot] = sum_re
        total_ref[1, slot] = sum_im


def finish_kernel(core_ref, own_ref, other_ref, own_image_ref, other_image_ref, out_ref, total_ref):
    core = core_ref[0]
    part_sums = []
    for part, image_ref in ((core, own_image_ref), (1 - core, other_image_ref)):
        sums = [jnp.zeros((HALF, LANES), jnp.float32)] * 4
        for slot in range(3):
            direction, residual = image_ref[0, slot], image_ref[1, slot]
            image_ap = own_ref[part, slot] + other_ref[part, slot] + damping_weight * direction
            total_ref[part, slot] = image_ap
            products = (residual * residual, direction * image_ap, residual * image_ap, image_ap * image_ap)
            sums = [a + b for a, b in zip(sums, products)]
        part_sums.append(sums)
    sums = [a + b for a, b in zip(*part_sums)]
    lane = lane_index(QUARTER)
    message = jnp.zeros((QUARTER, LANES), jnp.float32)
    for index, product in enumerate(sums):
        message = jnp.where(lane == SUMS_AT + index, jnp.sum(product), message)
    planes = out_ref.shape[0] // QUARTER
    own = 2 * 96 // planes
    rows = pl.ds(pl.multiple_of(core * QUARTER, QUARTER), QUARTER)
    lines = [[total_ref[part, slot, rows, :] for slot in range(3)] for part in range(2)]
    for c in range(planes):
        start = c * own
        block = message
        for part in range(2):
            for row in range(2):
                at = (2 * part + row) * own
                inside = (lane >= at) & (lane < at + own)
                if start < LANES:
                    block = jnp.where(inside, pltpu.roll(lines[part][row], (at - start) % LANES, 1), block)
                if start + own > LANES:
                    moved = pltpu.roll(lines[part][2], (at - (start - LANES + row * HALF)) % LANES, 1)
                    if start < LANES:
                        inside = inside & (lane >= at + LANES - start)
                    block = jnp.where(inside, moved, block)
        out_ref[c * QUARTER : (c + 1) * QUARTER, :] = block


def update_kernel(
    recv_ref, solution_ref, residual_ref, direction_ref, next_solution_ref, next_residual_ref, next_direction_ref
):
    own = direction_ref.shape[3]
    totals = jnp.sum(recv_ref[...], axis=0, keepdims=True)
    lane = lax.broadcasted_iota(jnp.int32, (1, LANES), 1)

    def pick(index):
        return jnp.sum(jnp.where(lane == SUMS_AT + index, totals, 0.0), axis=1, keepdims=True)

    norm_now, curvature, cross, square = pick(0), pick(1), pick(2), pick(3)
    alpha = norm_now / curvature
    fresh = jnp.maximum(norm_now + alpha * (alpha * square - 2.0 * cross), 0.0)
    beta = fresh / norm_now
    turned = recv_ref[...].T
    for part in range(2):
        for row in range(2):
            at = (2 * part + row) * own
            image_ap = turned[at : at + own]
            direction = direction_ref[part, 0, row]
            next_residual = residual_ref[part, 0, row] - alpha * image_ap
            next_solution_ref[part, 0, row] = solution_ref[part, 0, row] + alpha * direction
            next_residual_ref[part, 0, row] = next_residual
            next_direction_ref[part, 0, row] = next_residual + beta * direction


def normal_scratch(planes):
    return [
        pltpu.VMEM((2, 2, planes * HALF, 3 * LANES), jnp.bfloat16),
        pltpu.VMEM((2, planes, LANES, 3 * LANES), jnp.bfloat16),
        pltpu.VMEM((2, 3, HALF, LANES), jnp.float32),
    ]


def body(solution, residual, direction, sens_maps, sampling):
    axes = ("coil", "core", "chip")
    devices = lax.axis_size(axes)
    planes = lax.axis_size("coil")
    f32 = jnp.float32
    params = pltpu.CompilerParams(vmem_limit_bytes=24 * 1024 * 1024)
    hbm = pl.BlockSpec(memory_space=pl.ANY)
    whole = pl.BlockSpec(memory_space=pltpu.VMEM)
    packed = pl.pallas_call(
        pack_kernel,
        in_specs=[hbm] * 3,
        out_shape=jax.ShapeDtypeStruct((devices * ROWS, LANES), f32),
        scratch_shapes=[pltpu.VMEM(a.shape, f32) for a in (sens_maps, direction, residual)]
        + [pltpu.SemaphoreType.DMA((2, 2)), pltpu.SemaphoreType.DMA((2,))],
        compiler_params=params,
        name="pack",
    )(*(pltpu.with_memory_space_constraint(a, pltpu.HBM) for a in (sens_maps, direction, residual)))
    core = lax.axis_index("core").astype(jnp.int32).reshape(1)
    packed, core = lax.optimization_barrier((packed, core))
    moved = lax.all_to_all(packed.reshape(devices * ROWS, 1, LANES), axes, 0, 0, tiled=True)
    moved = moved.reshape(devices * ROWS, LANES)
    tables = [jnp.asarray(t) for t in make_tables(sampling.shape[1], sampling.shape[2])]
    swap = [(0, 1), (1, 0)]
    both = jax.ShapeDtypeStruct((2, 3, HALF, LANES), f32)
    image = pl.pallas_call(image_kernel, out_shape=both, compiler_params=params, name="image")(moved)
    other_image = lax.ppermute(image, "core", swap)
    scalar = pl.BlockSpec(memory_space=pltpu.SMEM)
    own = pl.pallas_call(
        normal_kernel,
        in_specs=[scalar] + [whole] * (4 + len(tables)),
        out_shape=both,
        scratch_shapes=normal_scratch(planes),
        compiler_params=params,
        name="normal",
    )(core, moved, image, other_image, sampling[0].T, *tables)
    other = lax.ppermute(own, "core", swap)
    chips = devices // 2
    result = pl.pallas_call(
        finish_kernel,
        in_specs=[scalar] + [whole] * 4,
        out_shape=jax.ShapeDtypeStruct((chips, LANES), f32),
        scratch_shapes=[pltpu.VMEM(both.shape, f32)],
        compiler_params=params,
        name="finish",
    )(core, own, other, image, other_image)
    home = lax.all_to_all(result.reshape(chips, 1, LANES), ("coil", "chip"), 0, 0, tiled=True).reshape(chips, LANES)
    out = jax.ShapeDtypeStruct(direction.shape, f32)
    return tuple(
        pl.pallas_call(update_kernel, out_shape=(out, out, out), compiler_params=params, name="update")(
            home, solution, residual, direction
        )
    )


def solution(mesh):
    planes, slabs = mesh.devices.shape
    split = Mesh(mesh.devices.reshape(planes, slabs // 2, 2), ("coil", "chip", "core"))
    image = P(None, None, ("chip", "core"), "coil", None)
    in_specs = (image, image, image, P(None, "coil", ("chip", "core"), None, None), P())
    return jax.shard_map(body, mesh=split, in_specs=in_specs, out_specs=(image, image, image), check_vma=False)
```

```python
import math

import jax
import jax.numpy as jnp
import ml_dtypes
import numpy as np
from jax import lax
from jax.experimental import pallas as pl
from jax.experimental.pallas import tpu as pltpu
from jax.sharding import Mesh
from jax.sharding import PartitionSpec as P

damping_weight = 0.5

LANES = 128
ROWS = 7
MESSAGE_IMAGE = 6
HALF = 64
QUARTER = 32
SUMS_AT = 96


def split_pair(table):
    high = table.astype(ml_dtypes.bfloat16)
    low = (table - high.astype(np.float64)).astype(ml_dtypes.bfloat16)
    return np.stack([high, low])


def angles(length):
    index = np.arange(length)
    angle = (index[:, None] * index[None, :] % length) * (2.0 * math.pi / length)
    scale = 1.0 / math.sqrt(length)
    return np.cos(angle) * scale, np.sin(angle) * scale


def make_tables(size_x, size_y):
    cos_y, sin_y = angles(size_y)
    cos_x, sin_x = angles(size_x)
    re_from_re = np.concatenate([cos_y[:, :LANES], -sin_y[:, :LANES], cos_y[:, LANES:], -sin_y[:, LANES:]], axis=1)
    re_from_im = np.concatenate([sin_y[:, :LANES], cos_y[:, :LANES], sin_y[:, LANES:], cos_y[:, LANES:]], axis=1)
    fwd_y = np.concatenate([re_from_re[:LANES], re_from_im[:LANES], re_from_re[LANES:], re_from_im[LANES:]], axis=0)
    order = np.arange(size_x).reshape(-1, 2, 2).transpose(2, 1, 0).reshape(-1)
    fwd_x = np.block([[cos_x[:, order], sin_x[:, order]], [-sin_x[:, order], cos_x[:, order]]])
    return [split_pair(t) for t in (fwd_y, fwd_y.T, fwd_x, fwd_x.T)]


def pack_kernel(maps_hbm, direction_hbm, residual_hbm, out_ref, maps_ref, direction_ref, residual_ref, maps_sem, image_sem):
    cells = maps_ref.shape[4]
    copies = [
        pltpu.make_async_copy(maps_hbm.at[part, core, row], maps_ref.at[part, core, row], maps_sem.at[part, core, row])
        for core in range(2)
        for part in range(2)
        for row in range(2)
    ]
    images = [
        pltpu.make_async_copy(direction_hbm, direction_ref, image_sem.at[0]),
        pltpu.make_async_copy(residual_hbm, residual_ref, image_sem.at[1]),
    ]
    for copy in images + copies:
        copy.start()

    def put(core, slot, block):
        turned = block.T
        for plane in range(cells // QUARTER):
            rows = pl.ds((plane * HALF + core * QUARTER) * ROWS + slot, QUARTER, stride=ROWS)
            out_ref[rows, :] = turned[plane * QUARTER : (plane + 1) * QUARTER]

    for copy in images:
        copy.wait()
    own = direction_ref.shape[3]
    filler = jnp.zeros((LANES - 4 * own, cells), jnp.float32)
    for core in range(2):
        pieces = [image_ref[core, 0, row] for image_ref in (direction_ref, residual_ref) for row in range(2)]
        put(core, MESSAGE_IMAGE, jnp.concatenate(pieces + [filler], axis=0))
    for core in range(2):
        for part in range(2):
            for row in range(2):
                copies[core * 4 + part * 2 + row].wait()
                put(core, part * 2 + row, maps_ref[part, core, row, :LANES, :])
            put(
                core,
                4 + part,
                jnp.concatenate([maps_ref[part, core, 0, LANES:, :], maps_ref[part, core, 1, LANES:, :]], axis=0),
            )


def lane_index(rows):
    return lax.broadcasted_iota(jnp.int32, (rows, LANES), 1)


def spread(blocks, own, slots):
    lane = lane_index(HALF)
    result = []
    for slot in slots:
        low = jnp.zeros((HALF, LANES), jnp.float32)
        high = jnp.zeros((HALF, LANES), jnp.float32)
        for c, block in enumerate(blocks):
            start = c * own
            moved = pltpu.roll(block, (start - slot * own) % LANES, 1)
            if start < LANES:
                low = jnp.where((lane >= start) & (lane < start + own), moved, low)
            if start + own > LANES:
                at = start - LANES
                high = jnp.where((lane >= at) & (lane < at + own), moved, high)
        result.append((low, high))
    return result


def join_low(first, second):
    return jnp.where(lane_index(HALF) < HALF, first, pltpu.roll(second, HALF, 1))


def join_high(first, second):
    return jnp.where(lane_index(HALF) < HALF, pltpu.roll(first, HALF, 1), second)


def halves(value):
    high = value.astype(jnp.bfloat16)
    low = (value - high.astype(jnp.float32)).astype(jnp.bfloat16)
    return high, low


def dot(a, b):
    return jnp.dot(a, b, preferred_element_type=jnp.float32)


def load_rows(recv_ref, c, slot):
    return recv_ref[pl.ds(c * HALF * ROWS + slot, HALF, stride=ROWS), :]


def image_kernel(recv_ref, image_ref):
    coils = recv_ref.shape[0] // (ROWS * HALF)
    own = 2 * 96 // coils
    pieces = spread([load_rows(recv_ref, c, MESSAGE_IMAGE) for c in range(coils)], own, range(4))
    for index in range(2):
        (low0, high0), (low1, high1) = pieces[2 * index], pieces[2 * index + 1]
        image_ref[index, 0] = low0
        image_ref[index, 1] = low1
        image_ref[index, 2] = join_low(high0, high1)


def normal_kernel(
    core_ref,
    recv_ref,
    own_image_ref,
    other_image_ref,
    weight_ref,
    fwd_y_ref,
    inv_y_ref,
    fwd_x_ref,
    inv_x_ref,
    total_ref,
    line_ref,
    mid_ref,
    image_ref,
):
    coils = recv_ref.shape[0] // (ROWS * HALF)
    core = core_ref[0]

    def load(c, slot):
        return load_rows(recv_ref, c, slot)

    image_ref[core] = own_image_ref[0]
    image_ref[1 - core] = other_image_ref[0]

    def store_line(row, c, column, value):
        for term, half in enumerate(halves(value)):
            at = (term * 3 + column) * LANES
            line_ref[row, c * HALF : (c + 1) * HALF, at : at + LANES] = half

    def along_y(row, table_ref):
        twice = jnp.concatenate([table_ref[0], table_ref[0]], axis=0)
        return dot(line_ref[row], twice) + dot(line_ref[row, :, : 3 * LANES], table_ref[1])

    for c in range(coils):
        for slot in range(3):
            s_re = load(c, slot if slot < 2 else 4)
            s_im = load(c, slot + 2 if slot < 2 else 5)
            d_re, d_im = image_ref[0, slot], image_ref[1, slot]
            x_re = s_re * d_re - s_im * d_im
            x_im = s_re * d_im + s_im * d_re
            if slot < 2:
                store_line(slot, c, 0, x_re)
                store_line(slot, c, 1, x_im)
            else:
                store_line(0, c, 2, join_low(x_re, x_im))
                store_line(1, c, 2, join_high(x_re, x_im))
    for row in range(2):
        spectra = along_y(row, fwd_y_ref)
        for pair in range(coils // 2):
            first, second = (spectra[c * HALF : (c + 1) * HALF] for c in (2 * pair, 2 * pair + 1))
            mixes = first[:, 2 * LANES :], second[:, 2 * LANES :]
            for part, join in enumerate((join_low, join_high)):
                at = (2 * part + row) * HALF
                columns = (
                    first[:, part * LANES : (part + 1) * LANES],
                    second[:, part * LANES : (part + 1) * LANES],
                    join(*mixes),
                )
                for column, value in enumerate(columns):
                    for term, half in enumerate(halves(value)):
                        mid_ref[term, pair, at : at + HALF, column * LANES : (column + 1) * LANES] = half
    weight_low = weight_ref[:LANES].astype(jnp.float32).T
    weight_high = weight_ref[LANES:].astype(jnp.float32).T
    weight = jnp.concatenate([weight_low, weight_low, jnp.concatenate([weight_high, weight_high], axis=1)], axis=1)
    weight = jnp.concatenate([weight, weight], axis=0)
    for pair in range(coils // 2):
        high, low = mid_ref[0, pair], mid_ref[1, pair]
        spectra = dot(fwd_x_ref[0], high) + (dot(fwd_x_ref[0], low) + dot(fwd_x_ref[1], high))
        high, low = halves(spectra * weight)
        value = dot(inv_x_ref[0], high) + (dot(inv_x_ref[0], low) + dot(inv_x_ref[1], high))
        for row in range(2):
            re, im = (value[(2 * part + row) * HALF : (2 * part + row + 1) * HALF] for part in range(2))
            mixes = re[:, 2 * LANES :], im[:, 2 * LANES :]
            for index, join in enumerate((join_low, join_high)):
                store_line(row, 2 * pair + index, 0, re[:, index * LANES : (index + 1) * LANES])
                store_line(row, 2 * pair + index, 1, im[:, index * LANES : (index + 1) * LANES])
                store_line(row, 2 * pair + index, 2, join(*mixes))
    lines = [along_y(row, inv_y_ref) for row in range(2)]
    for slot in range(3):
        sum_re = jnp.zeros((HALF, LANES), jnp.float32)
        sum_im = jnp.zeros((HALF, LANES), jnp.float32)
        for c in range(coils):
            rows = slice(c * HALF, (c + 1) * HALF)
            s_re = load(c, slot if slot < 2 else 4)
            s_im = load(c, slot + 2 if slot < 2 else 5)
            if slot < 2:
                y_re, y_im = lines[slot][rows, :LANES], lines[slot][rows, LANES : 2 * LANES]
            else:
                first, second = lines[0][rows, 2 * LANES :], lines[1][rows, 2 * LANES :]
                y_re, y_im = join_low(first, second), join_high(first, second)
            sum_re = sum_re + (s_re * y_re + s_im * y_im)
            sum_im = sum_im + (s_re * y_im - s_im * y_re)
        total_ref[0, slot] = sum_re
        total_ref[1, slot] = sum_im


def finish_kernel(core_ref, own_ref, other_ref, own_image_ref, other_image_ref, out_ref, total_ref):
    core = core_ref[0]
    part_sums = []
    for part, image_ref in ((core, own_image_ref), (1 - core, other_image_ref)):
        sums = [jnp.zeros((HALF, LANES), jnp.float32)] * 4
        for slot in range(3):
            direction, residual = image_ref[0, slot], image_ref[1, slot]
            image_ap = own_ref[part, slot] + other_ref[part, slot] + damping_weight * direction
            total_ref[part, slot] = image_ap
            products = (residual * residual, direction * image_ap, residual * image_ap, image_ap * image_ap)
            sums = [a + b for a, b in zip(sums, products)]
        part_sums.append(sums)
    sums = [a + b for a, b in zip(*part_sums)]
    lane = lane_index(QUARTER)
    message = jnp.zeros((QUARTER, LANES), jnp.float32)
    for index, product in enumerate(sums):
        message = jnp.where(lane == SUMS_AT + index, jnp.sum(product), message)
    planes = out_ref.shape[0] // QUARTER
    own = 2 * 96 // planes
    rows = pl.ds(pl.multiple_of(core * QUARTER, QUARTER), QUARTER)
    lines = [[total_ref[part, slot, rows, :] for slot in range(3)] for part in range(2)]
    for c in range(planes):
        start = c * own
        block = message
        for part in range(2):
            for row in range(2):
                at = (2 * part + row) * own
                inside = (lane >= at) & (lane < at + own)
                if start < LANES:
                    block = jnp.where(inside, pltpu.roll(lines[part][row], (at - start) % LANES, 1), block)
                if start + own > LANES:
                    moved = pltpu.roll(lines[part][2], (at - (start - LANES + row * HALF)) % LANES, 1)
                    if start < LANES:
                        inside = inside & (lane >= at + LANES - start)
                    block = jnp.where(inside, moved, block)
        out_ref[c * QUARTER : (c + 1) * QUARTER, :] = block


def update_kernel(
    recv_ref, solution_ref, residual_ref, direction_ref, next_solution_ref, next_residual_ref, next_direction_ref
):
    own = direction_ref.shape[3]
    totals = jnp.sum(recv_ref[...], axis=0, keepdims=True)
    lane = lax.broadcasted_iota(jnp.int32, (1, LANES), 1)

    def pick(index):
        return jnp.sum(jnp.where(lane == SUMS_AT + index, totals, 0.0), axis=1, keepdims=True)

    norm_now, curvature, cross, square = pick(0), pick(1), pick(2), pick(3)
    alpha = norm_now / curvature
    fresh = jnp.maximum(norm_now + alpha * (alpha * square - 2.0 * cross), 0.0)
    beta = fresh / norm_now
    turned = recv_ref[...].T
    for part in range(2):
        for row in range(2):
            at = (2 * part + row) * own
            image_ap = turned[at : at + own]
            direction = direction_ref[part, 0, row]
            next_residual = residual_ref[part, 0, row] - alpha * image_ap
            next_solution_ref[part, 0, row] = solution_ref[part, 0, row] + alpha * direction
            next_residual_ref[part, 0, row] = next_residual
            next_direction_ref[part, 0, row] = next_residual + beta * direction


def normal_scratch(planes):
    return [
        pltpu.VMEM((2, planes * HALF, 2 * 3 * LANES), jnp.bfloat16),
        pltpu.VMEM((2, planes // 2, 2 * LANES, 3 * LANES), jnp.bfloat16),
        pltpu.VMEM((2, 3, HALF, LANES), jnp.float32),
    ]


def body(solution, residual, direction, sens_maps, sampling):
    axes = ("coil", "core", "chip")
    devices = lax.axis_size(axes)
    planes = lax.axis_size("coil")
    f32 = jnp.float32
    params = pltpu.CompilerParams(vmem_limit_bytes=24 * 1024 * 1024)
    hbm = pl.BlockSpec(memory_space=pl.ANY)
    whole = pl.BlockSpec(memory_space=pltpu.VMEM)
    packed = pl.pallas_call(
        pack_kernel,
        in_specs=[hbm] * 3,
        out_shape=jax.ShapeDtypeStruct((devices * ROWS, LANES), f32),
        scratch_shapes=[pltpu.VMEM(a.shape, f32) for a in (sens_maps, direction, residual)]
        + [pltpu.SemaphoreType.DMA((2, 2, 2)), pltpu.SemaphoreType.DMA((2,))],
        compiler_params=params,
        name="pack",
    )(*(pltpu.with_memory_space_constraint(a, pltpu.HBM) for a in (sens_maps, direction, residual)))
    core = lax.axis_index("core").astype(jnp.int32).reshape(1)
    packed, core = lax.optimization_barrier((packed, core))
    moved = lax.all_to_all(packed.reshape(devices * ROWS, 1, LANES), axes, 0, 0, tiled=True)
    moved = moved.reshape(devices * ROWS, LANES)
    tables = [jnp.asarray(t) for t in make_tables(sampling.shape[1], sampling.shape[2])]
    swap = [(0, 1), (1, 0)]
    both = jax.ShapeDtypeStruct((2, 3, HALF, LANES), f32)
    image = pl.pallas_call(image_kernel, out_shape=both, compiler_params=params, name="image")(moved)
    other_image = lax.ppermute(image, "core", swap)
    scalar = pl.BlockSpec(memory_space=pltpu.SMEM)
    own = pl.pallas_call(
        normal_kernel,
        in_specs=[scalar] + [whole] * (4 + len(tables)),
        out_shape=both,
        scratch_shapes=normal_scratch(planes),
        compiler_params=params,
        name="normal",
    )(core, moved, image, other_image, sampling[0].T, *tables)
    other = lax.ppermute(own, "core", swap)
    chips = devices // 2
    result = pl.pallas_call(
        finish_kernel,
        in_specs=[scalar] + [whole] * 4,
        out_shape=jax.ShapeDtypeStruct((chips, LANES), f32),
        scratch_shapes=[pltpu.VMEM(both.shape, f32)],
        compiler_params=params,
        name="finish",
    )(core, own, other, image, other_image)
    home = lax.all_to_all(result.reshape(chips, 1, LANES), ("coil", "chip"), 0, 0, tiled=True).reshape(chips, LANES)
    out = jax.ShapeDtypeStruct(direction.shape, f32)
    return tuple(
        pl.pallas_call(update_kernel, out_shape=(out, out, out), compiler_params=params, name="update")(
            home, solution, residual, direction
        )
    )


def solution(mesh):
    planes, slabs = mesh.devices.shape
    split = Mesh(mesh.devices.reshape(planes, slabs // 2, 2), ("coil", "chip", "core"))
    image = P(None, None, ("chip", "core"), "coil", None)
    in_specs = (image, image, image, P(None, "coil", ("chip", "core"), None, None), P())
    return jax.shard_map(body, mesh=split, in_specs=in_specs, out_specs=(image, image, image), check_vma=False)
```

```python
import math

import jax
import jax.numpy as jnp
import ml_dtypes
import numpy as np
from jax import lax
from jax.experimental import pallas as pl
from jax.experimental.pallas import tpu as pltpu
from jax.sharding import Mesh
from jax.sharding import PartitionSpec as P

damping_weight = 0.5

LANES = 128
ROWS = 7
MESSAGE_IMAGE = 6
HALF = 64
QUARTER = 32
SUMS_AT = 96


def split_pair(table):
    high = table.astype(ml_dtypes.bfloat16)
    low = (table - high.astype(np.float64)).astype(ml_dtypes.bfloat16)
    return np.stack([high, low])


def angles(length):
    index = np.arange(length)
    angle = (index[:, None] * index[None, :] % length) * (2.0 * math.pi / length)
    scale = 1.0 / math.sqrt(length)
    return np.cos(angle) * scale, np.sin(angle) * scale


def make_tables(size_x, size_y):
    cos_y, sin_y = angles(size_y)
    cos_x, sin_x = angles(size_x)
    re_from_re = np.concatenate([cos_y[:, :LANES], -sin_y[:, :LANES], cos_y[:, LANES:], -sin_y[:, LANES:]], axis=1)
    re_from_im = np.concatenate([sin_y[:, :LANES], cos_y[:, :LANES], sin_y[:, LANES:], cos_y[:, LANES:]], axis=1)
    fwd_y = np.concatenate([re_from_re[:LANES], re_from_im[:LANES], re_from_re[LANES:], re_from_im[LANES:]], axis=0)
    order = np.arange(size_x).reshape(-1, 2, 2).transpose(2, 1, 0).reshape(-1)
    fwd_x = np.block([[cos_x[:, order], sin_x[:, order]], [-sin_x[:, order], cos_x[:, order]]])
    fwd_x = fwd_x.reshape(2 * size_x, 2, 2, HALF).transpose(0, 2, 1, 3).reshape(2 * size_x, 2 * size_x)
    return [split_pair(t) for t in (fwd_y, fwd_y.T, fwd_x, fwd_x.T)]


def pack_kernel(maps_hbm, direction_hbm, residual_hbm, out_ref, maps_ref, direction_ref, residual_ref, maps_sem, image_sem):
    cells = maps_ref.shape[4]
    copies = [
        pltpu.make_async_copy(maps_hbm.at[:, core], maps_ref.at[:, core], maps_sem.at[core]) for core in range(2)
    ]
    images = [
        pltpu.make_async_copy(direction_hbm, direction_ref, image_sem.at[0]),
        pltpu.make_async_copy(residual_hbm, residual_ref, image_sem.at[1]),
    ]
    for copy in copies + images:
        copy.start()

    def put(core, slot, block):
        turned = block.T
        for plane in range(cells // QUARTER):
            rows = pl.ds((plane * HALF + core * QUARTER) * ROWS + slot, QUARTER, stride=ROWS)
            out_ref[rows, :] = turned[plane * QUARTER : (plane + 1) * QUARTER]

    for core in range(2):
        copies[core].wait()
        for part in range(2):
            for row in range(2):
                put(core, part * 2 + row, maps_ref[part, core, row, :LANES, :])
            put(
                core,
                4 + part,
                jnp.concatenate([maps_ref[part, core, 0, LANES:, :], maps_ref[part, core, 1, LANES:, :]], axis=0),
            )
    for copy in images:
        copy.wait()
    filler = jnp.zeros((LANES - 5 * direction_ref.shape[3], cells), jnp.float32)
    for core in range(2):
        pieces = [direction_ref[0, 0, 0], direction_ref[1, 0, 0], direction_ref[core, 0, 1]]
        pieces += [residual_ref[core, 0, 0], residual_ref[core, 0, 1], filler]
        put(core, MESSAGE_IMAGE, jnp.concatenate(pieces, axis=0))


def lane_index(rows):
    return lax.broadcasted_iota(jnp.int32, (rows, LANES), 1)


def spread(blocks, own, slots):
    lane = lane_index(HALF)
    result = []
    for slot in slots:
        low = jnp.zeros((HALF, LANES), jnp.float32)
        high = jnp.zeros((HALF, LANES), jnp.float32)
        for c, block in enumerate(blocks):
            start = c * own
            moved = pltpu.roll(block, (start - slot * own) % LANES, 1)
            if start < LANES:
                low = jnp.where((lane >= start) & (lane < start + own), moved, low)
            if start + own > LANES:
                at = start - LANES
                high = jnp.where((lane >= at) & (lane < at + own), moved, high)
        result.append((low, high))
    return result


def join_low(first, second):
    return jnp.where(lane_index(HALF) < HALF, first, pltpu.roll(second, HALF, 1))


def join_high(first, second):
    return jnp.where(lane_index(HALF) < HALF, pltpu.roll(first, HALF, 1), second)


def halves(value):
    high = value.astype(jnp.bfloat16)
    low = (value - high.astype(jnp.float32)).astype(jnp.bfloat16)
    return high, low


def dot(a, b):
    return jnp.dot(a, b, preferred_element_type=jnp.float32)


def load_rows(recv_ref, c, slot):
    return recv_ref[pl.ds(c * HALF * ROWS + slot, HALF, stride=ROWS), :]


def image_kernel(recv_ref, first_ref, rest_ref):
    coils = recv_ref.shape[0] // (ROWS * HALF)
    own = 2 * 96 // coils
    lines = spread([load_rows(recv_ref, c, MESSAGE_IMAGE) for c in range(coils)], own, range(5))
    for part in range(2):
        for index in range(2):
            first_ref[part, index] = lines[part][index]
    for index in range(3):
        rest_ref[index] = lines[2 + index][0]
    rest_ref[3] = join_low(lines[3][1], lines[4][1])
    rest_ref[4] = pltpu.roll(lines[2][1], HALF, 1)


def store_halves(line_ref, c, column, value):
    for term, half in enumerate(halves(value)):
        at = (term * 3 + column) * LANES
        line_ref[c * HALF : (c + 1) * HALF, at : at + LANES] = half


def along_y(line_ref, table_ref):
    twice = jnp.concatenate([table_ref[0], table_ref[0]], axis=0)
    return dot(line_ref[...], twice) + dot(line_ref[:, : 3 * LANES], table_ref[1])


def forward_y(recv_ref, row, image_ref, table_ref, line_ref, mid_ref):
    coils = recv_ref.shape[0] // (ROWS * HALF)
    join = join_high if row else join_low
    for c in range(coils):
        products = []
        for index, slot in enumerate((row, 4)):
            s_re = load_rows(recv_ref, c, slot)
            s_im = load_rows(recv_ref, c, slot + 1 if slot == 4 else slot + 2)
            d_re, d_im = image_ref[0, index], image_ref[1, index]
            products.append((s_re * d_re - s_im * d_im, s_re * d_im + s_im * d_re))
        store_halves(line_ref, c, 0, products[0][0])
        store_halves(line_ref, c, 1, products[0][1])
        store_halves(line_ref, c, 2, join(*products[1]))
    spectra = along_y(line_ref, table_ref)
    for pair in range(coils // 2):
        first, second = (spectra[c * HALF : (c + 1) * HALF] for c in (2 * pair, 2 * pair + 1))
        mixes = first[:, 2 * LANES :], second[:, 2 * LANES :]
        for part, join_part in enumerate((join_low, join_high)):
            columns = (
                first[:, part * LANES : (part + 1) * LANES],
                second[:, part * LANES : (part + 1) * LANES],
                join_part(*mixes),
            )
            for column, value in enumerate(columns):
                for term, half in enumerate(halves(value)):
                    rows = slice(part * HALF, (part + 1) * HALF)
                    mid_ref[term, pair, rows, column * LANES : (column + 1) * LANES] = half


def first_kernel(recv_ref, first_ref, fwd_y_ref, mid_ref, line_ref):
    forward_y(recv_ref, 0, first_ref, fwd_y_ref, line_ref, mid_ref)


def normal_kernel(
    core_ref,
    recv_ref,
    own_rest_ref,
    other_rest_ref,
    first_mid_ref,
    weight_ref,
    fwd_y_ref,
    inv_y_ref,
    fwd_x_ref,
    inv_x_ref,
    total_ref,
    line_ref,
    mid_ref,
    image_ref,
):
    coils = recv_ref.shape[0] // (ROWS * HALF)
    core = core_ref[0]

    def load(c, slot):
        return load_rows(recv_ref, c, slot)

    for part, rest_ref in ((core, own_rest_ref), (1 - core, other_rest_ref)):
        image_ref[part, 0] = rest_ref[0]
        image_ref[part, 1] = rest_ref[4]
    forward_y(recv_ref, 1, image_ref, fwd_y_ref, line_ref.at[1], mid_ref)
    weight_low = weight_ref[:LANES].astype(jnp.float32).T
    weight_high = weight_ref[LANES:].astype(jnp.float32).T
    weight = jnp.concatenate([weight_low, weight_low, jnp.concatenate([weight_high, weight_high], axis=1)], axis=1)
    weight = jnp.concatenate([weight, weight], axis=0)
    for pair in range(coils // 2):
        high, low = (jnp.concatenate([first_mid_ref[term, pair], mid_ref[term, pair]], axis=0) for term in range(2))
        spectra = dot(fwd_x_ref[0], high) + (dot(fwd_x_ref[0], low) + dot(fwd_x_ref[1], high))
        high, low = halves(spectra * weight)
        value = dot(inv_x_ref[0], high) + (dot(inv_x_ref[0], low) + dot(inv_x_ref[1], high))
        for row in range(2):
            re, im = (value[(2 * row + part) * HALF : (2 * row + part + 1) * HALF] for part in range(2))
            mixes = re[:, 2 * LANES :], im[:, 2 * LANES :]
            for index, join in enumerate((join_low, join_high)):
                columns = re, im
                for column, value_part in enumerate(columns):
                    lanes = slice(index * LANES, (index + 1) * LANES)
                    store_halves(line_ref.at[row], 2 * pair + index, column, value_part[:, lanes])
                store_halves(line_ref.at[row], 2 * pair + index, 2, join(*mixes))
    lines = [along_y(line_ref.at[row], inv_y_ref) for row in range(2)]
    for slot in range(3):
        sum_re = jnp.zeros((HALF, LANES), jnp.float32)
        sum_im = jnp.zeros((HALF, LANES), jnp.float32)
        for c in range(coils):
            rows = slice(c * HALF, (c + 1) * HALF)
            s_re = load(c, slot if slot < 2 else 4)
            s_im = load(c, slot + 2 if slot < 2 else 5)
            if slot < 2:
                y_re, y_im = lines[slot][rows, :LANES], lines[slot][rows, LANES : 2 * LANES]
            else:
                first, second = lines[0][rows, 2 * LANES :], lines[1][rows, 2 * LANES :]
                y_re, y_im = join_low(first, second), join_high(first, second)
            sum_re = sum_re + (s_re * y_re + s_im * y_im)
            sum_im = sum_im + (s_re * y_im - s_im * y_re)
        total_ref[0, slot] = sum_re
        total_ref[1, slot] = sum_im


def finish_kernel(core_ref, own_ref, other_ref, first_ref, own_rest_ref, other_rest_ref, out_ref, total_ref):
    core = core_ref[0]
    part_sums = []
    below = lane_index(HALF) < HALF
    for part, rest_ref in ((core, own_rest_ref), (1 - core, other_rest_ref)):
        sums = [jnp.zeros((HALF, LANES), jnp.float32)] * 4
        for slot in range(3):
            residual = rest_ref[slot + 1]
            if slot == 0:
                direction = first_ref[part, 0]
            elif slot == 1:
                direction = rest_ref[0]
            else:
                direction = jnp.where(below, first_ref[part, 1], rest_ref[4])
            image_ap = own_ref[part, slot] + other_ref[part, slot] + damping_weight * direction
            total_ref[part, slot] = image_ap
            products = (residual * residual, direction * image_ap, residual * image_ap, image_ap * image_ap)
            sums = [a + b for a, b in zip(sums, products)]
        part_sums.append(sums)
    sums = [a + b for a, b in zip(*part_sums)]
    lane = lane_index(QUARTER)
    message = jnp.zeros((QUARTER, LANES), jnp.float32)
    for index, product in enumerate(sums):
        message = jnp.where(lane == SUMS_AT + index, jnp.sum(product), message)
    planes = out_ref.shape[0] // QUARTER
    own = 2 * 96 // planes
    rows = pl.ds(pl.multiple_of(core * QUARTER, QUARTER), QUARTER)
    lines = [[total_ref[part, slot, rows, :] for slot in range(3)] for part in range(2)]
    for c in range(planes):
        start = c * own
        block = message
        for part in range(2):
            for row in range(2):
                at = (2 * part + row) * own
                inside = (lane >= at) & (lane < at + own)
                if start < LANES:
                    block = jnp.where(inside, pltpu.roll(lines[part][row], (at - start) % LANES, 1), block)
                if start + own > LANES:
                    moved = pltpu.roll(lines[part][2], (at - (start - LANES + row * HALF)) % LANES, 1)
                    if start < LANES:
                        inside = inside & (lane >= at + LANES - start)
                    block = jnp.where(inside, moved, block)
        out_ref[c * QUARTER : (c + 1) * QUARTER, :] = block


def update_kernel(
    recv_ref, solution_ref, residual_ref, direction_ref, next_solution_ref, next_residual_ref, next_direction_ref
):
    own = direction_ref.shape[3]
    totals = jnp.sum(recv_ref[...], axis=0, keepdims=True)
    lane = lax.broadcasted_iota(jnp.int32, (1, LANES), 1)

    def pick(index):
        return jnp.sum(jnp.where(lane == SUMS_AT + index, totals, 0.0), axis=1, keepdims=True)

    norm_now, curvature, cross, square = pick(0), pick(1), pick(2), pick(3)
    alpha = norm_now / curvature
    fresh = jnp.maximum(norm_now + alpha * (alpha * square - 2.0 * cross), 0.0)
    beta = fresh / norm_now
    turned = recv_ref[...].T
    for part in range(2):
        for row in range(2):
            at = (2 * part + row) * own
            image_ap = turned[at : at + own]
            direction = direction_ref[part, 0, row]
            next_residual = residual_ref[part, 0, row] - alpha * image_ap
            next_solution_ref[part, 0, row] = solution_ref[part, 0, row] + alpha * direction
            next_residual_ref[part, 0, row] = next_residual
            next_direction_ref[part, 0, row] = next_residual + beta * direction


def normal_scratch(planes):
    return [
        pltpu.VMEM((2, planes * HALF, 2 * 3 * LANES), jnp.bfloat16),
        pltpu.VMEM((2, planes // 2, LANES, 3 * LANES), jnp.bfloat16),
        pltpu.VMEM((2, 2, HALF, LANES), jnp.float32),
    ]


def body(solution, residual, direction, sens_maps, sampling):
    axes = ("coil", "core", "chip")
    devices = lax.axis_size(axes)
    planes = lax.axis_size("coil")
    f32 = jnp.float32
    params = pltpu.CompilerParams(vmem_limit_bytes=24 * 1024 * 1024)
    hbm = pl.BlockSpec(memory_space=pl.ANY)
    whole = pl.BlockSpec(memory_space=pltpu.VMEM)
    packed = pl.pallas_call(
        pack_kernel,
        in_specs=[hbm] * 3,
        out_shape=jax.ShapeDtypeStruct((devices * ROWS, LANES), f32),
        scratch_shapes=[pltpu.VMEM(a.shape, f32) for a in (sens_maps, direction, residual)]
        + [pltpu.SemaphoreType.DMA((2,)), pltpu.SemaphoreType.DMA((2,))],
        compiler_params=params,
        name="pack",
    )(*(pltpu.with_memory_space_constraint(a, pltpu.HBM) for a in (sens_maps, direction, residual)))
    core = lax.axis_index("core").astype(jnp.int32).reshape(1)
    packed, core = lax.optimization_barrier((packed, core))
    moved = lax.all_to_all(packed.reshape(devices * ROWS, 1, LANES), axes, 0, 0, tiled=True)
    moved = moved.reshape(devices * ROWS, LANES)
    tables = [jnp.asarray(t) for t in make_tables(sampling.shape[1], sampling.shape[2])]
    swap = [(0, 1), (1, 0)]
    both = jax.ShapeDtypeStruct((2, 3, HALF, LANES), f32)
    first, rest = pl.pallas_call(
        image_kernel,
        out_shape=(jax.ShapeDtypeStruct((2, 2, HALF, LANES), f32), jax.ShapeDtypeStruct((5, HALF, LANES), f32)),
        compiler_params=params,
        name="image",
    )(moved)
    other_rest = lax.ppermute(rest, "core", swap)
    first_mid = pl.pallas_call(
        first_kernel,
        out_shape=jax.ShapeDtypeStruct((2, planes // 2, LANES, 3 * LANES), jnp.bfloat16),
        scratch_shapes=[pltpu.VMEM((planes * HALF, 2 * 3 * LANES), jnp.bfloat16)],
        compiler_params=params,
        name="first",
    )(moved, first, tables[0])
    scalar = pl.BlockSpec(memory_space=pltpu.SMEM)
    own = pl.pallas_call(
        normal_kernel,
        in_specs=[scalar] + [whole] * (5 + len(tables)),
        out_shape=both,
        scratch_shapes=normal_scratch(planes),
        compiler_params=params,
        name="normal",
    )(core, moved, rest, other_rest, first_mid, sampling[0].T, *tables)
    other = lax.ppermute(own, "core", swap)
    chips = devices // 2
    result = pl.pallas_call(
        finish_kernel,
        in_specs=[scalar] + [whole] * 5,
        out_shape=jax.ShapeDtypeStruct((chips, LANES), f32),
        scratch_shapes=[pltpu.VMEM(both.shape, f32)],
        compiler_params=params,
        name="finish",
    )(core, own, other, first, rest, other_rest)
    home = lax.all_to_all(result.reshape(chips, 1, LANES), ("coil", "chip"), 0, 0, tiled=True).reshape(chips, LANES)
    out = jax.ShapeDtypeStruct(direction.shape, f32)
    return tuple(
        pl.pallas_call(update_kernel, out_shape=(out, out, out), compiler_params=params, name="update")(
            home, solution, residual, direction
        )
    )


def solution(mesh):
    planes, slabs = mesh.devices.shape
    split = Mesh(mesh.devices.reshape(planes, slabs // 2, 2), ("coil", "chip", "core"))
    image = P(None, None, ("chip", "core"), "coil", None)
    in_specs = (image, image, image, P(None, "coil", ("chip", "core"), None, None), P())
    return jax.shard_map(body, mesh=split, in_specs=in_specs, out_specs=(image, image, image), check_vma=False)
```

```python
import math

import jax
import jax.numpy as jnp
import ml_dtypes
import numpy as np
from jax import lax
from jax.experimental import pallas as pl
from jax.experimental.pallas import tpu as pltpu
from jax.sharding import Mesh
from jax.sharding import PartitionSpec as P

damping_weight = 0.5

LANES = 128
ROWS = 7
MESSAGE_IMAGE = 6
HALF = 64
QUARTER = 32
EIGHT = 8
SUMS_AT = 96


def split_pair(table):
    high = table.astype(ml_dtypes.bfloat16)
    low = (table - high.astype(np.float64)).astype(ml_dtypes.bfloat16)
    return np.stack([high, low])


def angles(length):
    index = np.arange(length)
    angle = (index[:, None] * index[None, :] % length) * (2.0 * math.pi / length)
    scale = 1.0 / math.sqrt(length)
    return np.cos(angle) * scale, np.sin(angle) * scale


def make_tables(size_x, size_y):
    cos_y, sin_y = angles(size_y)
    cos_x, sin_x = angles(size_x)
    re_from_re = np.concatenate([cos_y[:, :LANES], -sin_y[:, :LANES], cos_y[:, LANES:], -sin_y[:, LANES:]], axis=1)
    re_from_im = np.concatenate([sin_y[:, :LANES], cos_y[:, :LANES], sin_y[:, LANES:], cos_y[:, LANES:]], axis=1)
    fwd_y = np.concatenate([re_from_re[:LANES], re_from_im[:LANES], re_from_re[LANES:], re_from_im[LANES:]], axis=0)
    order = np.arange(size_x).reshape(EIGHT, -1, 2, 2).transpose(3, 0, 2, 1).reshape(-1)
    fwd_x = np.block([[cos_x[:, order], sin_x[:, order]], [-sin_x[:, order], cos_x[:, order]]])
    fwd_x = fwd_x.reshape(2 * size_x, 2, 2, HALF).transpose(0, 2, 1, 3).reshape(2 * size_x, 2 * size_x)
    return [split_pair(t) for t in (fwd_y, fwd_y.T, fwd_x, fwd_x.T)]


def pack_kernel(maps_hbm, direction_hbm, residual_hbm, out_ref, maps_ref, direction_ref, residual_ref, maps_sem, image_sem):
    cells = maps_ref.shape[4]
    copies = [
        pltpu.make_async_copy(maps_hbm.at[:, core], maps_ref.at[:, core], maps_sem.at[core]) for core in range(2)
    ]
    images = [
        pltpu.make_async_copy(direction_hbm, direction_ref, image_sem.at[0]),
        pltpu.make_async_copy(residual_hbm, residual_ref, image_sem.at[1]),
    ]
    for copy in copies + images:
        copy.start()

    def put(core, slot, block):
        turned = block.T
        for place in range(4):
            rows = pl.ds((core * 4 + place) * ROWS + slot, cells // 4, stride=EIGHT * ROWS)
            out_ref[rows, :] = turned[place * (cells // 4) : (place + 1) * (cells // 4)]

    for core in range(2):
        copies[core].wait()
        for part in range(2):
            for row in range(2):
                put(core, part * 2 + row, maps_ref[part, core, row, :LANES, :])
            put(
                core,
                4 + part,
                jnp.concatenate([maps_ref[part, core, 0, LANES:, :], maps_ref[part, core, 1, LANES:, :]], axis=0),
            )
    for copy in images:
        copy.wait()
    filler = jnp.zeros((LANES - 5 * direction_ref.shape[3], cells), jnp.float32)
    for core in range(2):
        pieces = [direction_ref[0, 0, 0], direction_ref[1, 0, 0], direction_ref[core, 0, 1]]
        pieces += [residual_ref[core, 0, 0], residual_ref[core, 0, 1], filler]
        put(core, MESSAGE_IMAGE, jnp.concatenate(pieces, axis=0))


def lane_index(rows):
    return lax.broadcasted_iota(jnp.int32, (rows, LANES), 1)


def spread(blocks, own, slots):
    lane = lane_index(HALF)
    result = []
    for slot in slots:
        low = jnp.zeros((HALF, LANES), jnp.float32)
        high = jnp.zeros((HALF, LANES), jnp.float32)
        for c, block in enumerate(blocks):
            start = c * own
            moved = pltpu.roll(block, (start - slot * own) % LANES, 1)
            if start < LANES:
                low = jnp.where((lane >= start) & (lane < start + own), moved, low)
            if start + own > LANES:
                at = start - LANES
                high = jnp.where((lane >= at) & (lane < at + own), moved, high)
        result.append((low, high))
    return result


def join_low(first, second):
    return jnp.where(lane_index(HALF) < HALF, first, pltpu.roll(second, HALF, 1))


def join_high(first, second):
    return jnp.where(lane_index(HALF) < HALF, pltpu.roll(first, HALF, 1), second)


def halves(value):
    high = value.astype(jnp.bfloat16)
    low = (value - high.astype(jnp.float32)).astype(jnp.bfloat16)
    return high, low


def dot(a, b):
    return jnp.dot(a, b, preferred_element_type=jnp.float32)


def load_rows(recv_ref, c, slot):
    starts = ((line * EIGHT + c) * EIGHT * ROWS + slot for line in range(EIGHT))
    return jnp.concatenate([recv_ref[pl.ds(start, EIGHT, stride=ROWS), :] for start in starts], axis=0)


def image_kernel(recv_ref, first_ref, rest_ref):
    coils = recv_ref.shape[0] // (ROWS * HALF)
    own = 2 * 96 // coils
    lines = spread([load_rows(recv_ref, c, MESSAGE_IMAGE) for c in range(coils)], own, range(5))
    for part in range(2):
        for index in range(2):
            first_ref[part, index] = lines[part][index]
    for index in range(3):
        rest_ref[index] = lines[2 + index][0]
    rest_ref[3] = join_low(lines[3][1], lines[4][1])
    rest_ref[4] = pltpu.roll(lines[2][1], HALF, 1)


def store_halves(line_ref, c, column, value):
    for term, half in enumerate(halves(value)):
        at = (term * 3 + column) * LANES
        line_ref[c * HALF : (c + 1) * HALF, at : at + LANES] = half


def along_y(line_ref, table_ref):
    twice = jnp.concatenate([table_ref[0], table_ref[0]], axis=0)
    return dot(line_ref[...], twice) + dot(line_ref[:, : 3 * LANES], table_ref[1])


def forward_y(recv_ref, row, image_ref, table_ref, line_ref, mid_ref):
    coils = recv_ref.shape[0] // (ROWS * HALF)
    join = join_high if row else join_low
    for c in range(coils):
        products = []
        for index, slot in enumerate((row, 4)):
            s_re = load_rows(recv_ref, c, slot)
            s_im = load_rows(recv_ref, c, slot + 1 if slot == 4 else slot + 2)
            d_re, d_im = image_ref[0, index], image_ref[1, index]
            products.append((s_re * d_re - s_im * d_im, s_re * d_im + s_im * d_re))
        store_halves(line_ref, c, 0, products[0][0])
        store_halves(line_ref, c, 1, products[0][1])
        store_halves(line_ref, c, 2, join(*products[1]))
    spectra = along_y(line_ref, table_ref)
    for pair in range(coils // 2):
        first, second = (spectra[c * HALF : (c + 1) * HALF] for c in (2 * pair, 2 * pair + 1))
        mixes = first[:, 2 * LANES :], second[:, 2 * LANES :]
        for part, join_part in enumerate((join_low, join_high)):
            columns = (
                first[:, part * LANES : (part + 1) * LANES],
                second[:, part * LANES : (part + 1) * LANES],
                join_part(*mixes),
            )
            for column, value in enumerate(columns):
                for term, half in enumerate(halves(value)):
                    rows = slice(part * HALF, (part + 1) * HALF)
                    mid_ref[term, pair, rows, column * LANES : (column + 1) * LANES] = half


def first_kernel(recv_ref, first_ref, fwd_y_ref, mid_ref, line_ref):
    forward_y(recv_ref, 0, first_ref, fwd_y_ref, line_ref, mid_ref)


def normal_kernel(
    core_ref,
    recv_ref,
    own_rest_ref,
    other_rest_ref,
    first_mid_ref,
    weight_ref,
    fwd_y_ref,
    inv_y_ref,
    fwd_x_ref,
    inv_x_ref,
    total_ref,
    line_ref,
    mid_ref,
    image_ref,
):
    coils = recv_ref.shape[0] // (ROWS * HALF)
    core = core_ref[0]

    def load(c, slot):
        return load_rows(recv_ref, c, slot)

    for part, rest_ref in ((core, own_rest_ref), (1 - core, other_rest_ref)):
        image_ref[part, 0] = rest_ref[0]
        image_ref[part, 1] = rest_ref[4]
    forward_y(recv_ref, 1, image_ref, fwd_y_ref, line_ref.at[1], mid_ref)
    weight_low = weight_ref[:LANES].astype(jnp.float32).T
    weight_high = weight_ref[LANES:].astype(jnp.float32).T
    weight = jnp.concatenate([weight_low, weight_low, jnp.concatenate([weight_high, weight_high], axis=1)], axis=1)
    weight = jnp.concatenate([weight, weight], axis=0)
    for pair in range(coils // 2):
        high, low = (jnp.concatenate([first_mid_ref[term, pair], mid_ref[term, pair]], axis=0) for term in range(2))
        spectra = dot(fwd_x_ref[0], high) + (dot(fwd_x_ref[0], low) + dot(fwd_x_ref[1], high))
        high, low = halves(spectra * weight)
        value = dot(inv_x_ref[0], high) + (dot(inv_x_ref[0], low) + dot(inv_x_ref[1], high))
        for row in range(2):
            re, im = (value[(2 * row + part) * HALF : (2 * row + part + 1) * HALF] for part in range(2))
            mixes = re[:, 2 * LANES :], im[:, 2 * LANES :]
            for index, join in enumerate((join_low, join_high)):
                columns = re, im
                for column, value_part in enumerate(columns):
                    lanes = slice(index * LANES, (index + 1) * LANES)
                    store_halves(line_ref.at[row], 2 * pair + index, column, value_part[:, lanes])
                store_halves(line_ref.at[row], 2 * pair + index, 2, join(*mixes))
    lines = [along_y(line_ref.at[row], inv_y_ref) for row in range(2)]
    for slot in range(3):
        sum_re = jnp.zeros((HALF, LANES), jnp.float32)
        sum_im = jnp.zeros((HALF, LANES), jnp.float32)
        for c in range(coils):
            rows = slice(c * HALF, (c + 1) * HALF)
            s_re = load(c, slot if slot < 2 else 4)
            s_im = load(c, slot + 2 if slot < 2 else 5)
            if slot < 2:
                y_re, y_im = lines[slot][rows, :LANES], lines[slot][rows, LANES : 2 * LANES]
            else:
                first, second = lines[0][rows, 2 * LANES :], lines[1][rows, 2 * LANES :]
                y_re, y_im = join_low(first, second), join_high(first, second)
            sum_re = sum_re + (s_re * y_re + s_im * y_im)
            sum_im = sum_im + (s_re * y_im - s_im * y_re)
        total_ref[0, slot] = sum_re
        total_ref[1, slot] = sum_im


def finish_kernel(core_ref, own_ref, other_ref, first_ref, own_rest_ref, other_rest_ref, out_ref, total_ref):
    core = core_ref[0]
    part_sums = []
    below = lane_index(HALF) < HALF
    for part, rest_ref in ((core, own_rest_ref), (1 - core, other_rest_ref)):
        sums = [jnp.zeros((HALF, LANES), jnp.float32)] * 4
        for slot in range(3):
            residual = rest_ref[slot + 1]
            if slot == 0:
                direction = first_ref[part, 0]
            elif slot == 1:
                direction = rest_ref[0]
            else:
                direction = jnp.where(below, first_ref[part, 1], rest_ref[4])
            image_ap = own_ref[part, slot] + other_ref[part, slot] + damping_weight * direction
            total_ref[pl.ds(pl.multiple_of((part * 3 + slot) * HALF, HALF), HALF), :] = image_ap
            products = (residual * residual, direction * image_ap, residual * image_ap, image_ap * image_ap)
            sums = [a + b for a, b in zip(sums, products)]
        part_sums.append(sums)
    sums = [a + b for a, b in zip(*part_sums)]
    lane = lane_index(QUARTER)
    message = jnp.zeros((QUARTER, LANES), jnp.float32)
    for index, product in enumerate(sums):
        message = jnp.where(lane == SUMS_AT + index, jnp.sum(product), message)
    planes = out_ref.shape[0] // QUARTER
    own = 2 * 96 // planes

    def owned(part, slot):
        base = (part * 3 + slot) * HALF
        first, second = (
            jnp.concatenate(
                [total_ref[pl.ds(base + index * 4 + place, EIGHT, stride=EIGHT), :] for place in range(4)], axis=0
            )
            for index in range(2)
        )
        return jnp.where(core == 0, first, second)

    lines = [[owned(part, slot) for slot in range(3)] for part in range(2)]
    for c in range(planes):
        start = c * own
        block = message
        for part in range(2):
            for row in range(2):
                at = (2 * part + row) * own
                inside = (lane >= at) & (lane < at + own)
                if start < LANES:
                    block = jnp.where(inside, pltpu.roll(lines[part][row], (at - start) % LANES, 1), block)
                if start + own > LANES:
                    moved = pltpu.roll(lines[part][2], (at - (start - LANES + row * HALF)) % LANES, 1)
                    if start < LANES:
                        inside = inside & (lane >= at + LANES - start)
                    block = jnp.where(inside, moved, block)
        for place in range(4):
            out_ref[pl.ds(place * HALF + c, EIGHT, stride=EIGHT), :] = block[place * EIGHT : (place + 1) * EIGHT]


def update_kernel(
    recv_ref, solution_ref, residual_ref, direction_ref, next_solution_ref, next_residual_ref, next_direction_ref
):
    own = direction_ref.shape[3]
    totals = jnp.sum(recv_ref[...], axis=0, keepdims=True)
    lane = lax.broadcasted_iota(jnp.int32, (1, LANES), 1)

    def pick(index):
        return jnp.sum(jnp.where(lane == SUMS_AT + index, totals, 0.0), axis=1, keepdims=True)

    norm_now, curvature, cross, square = pick(0), pick(1), pick(2), pick(3)
    alpha = norm_now / curvature
    fresh = jnp.maximum(norm_now + alpha * (alpha * square - 2.0 * cross), 0.0)
    beta = fresh / norm_now
    turned = recv_ref[...].T
    for part in range(2):
        for row in range(2):
            at = (2 * part + row) * own
            image_ap = turned[at : at + own]
            direction = direction_ref[part, 0, row]
            next_residual = residual_ref[part, 0, row] - alpha * image_ap
            next_solution_ref[part, 0, row] = solution_ref[part, 0, row] + alpha * direction
            next_residual_ref[part, 0, row] = next_residual
            next_direction_ref[part, 0, row] = next_residual + beta * direction


def normal_scratch(planes):
    return [
        pltpu.VMEM((2, planes * HALF, 2 * 3 * LANES), jnp.bfloat16),
        pltpu.VMEM((2, planes // 2, LANES, 3 * LANES), jnp.bfloat16),
        pltpu.VMEM((2, 2, HALF, LANES), jnp.float32),
    ]


def body(solution, residual, direction, sens_maps, sampling):
    chip_axes = ("place", "line", "coil")
    axes = ("line", "coil", "core", "place")
    devices = lax.axis_size(axes)
    planes = lax.axis_size("coil")
    f32 = jnp.float32
    params = pltpu.CompilerParams(vmem_limit_bytes=24 * 1024 * 1024)
    hbm = pl.BlockSpec(memory_space=pl.ANY)
    whole = pl.BlockSpec(memory_space=pltpu.VMEM)
    packed = pl.pallas_call(
        pack_kernel,
        in_specs=[hbm] * 3,
        out_shape=jax.ShapeDtypeStruct((devices * ROWS, LANES), f32),
        scratch_shapes=[pltpu.VMEM(a.shape, f32) for a in (sens_maps, direction, residual)]
        + [pltpu.SemaphoreType.DMA((2,)), pltpu.SemaphoreType.DMA((2,))],
        compiler_params=params,
        name="pack",
    )(*(pltpu.with_memory_space_constraint(a, pltpu.HBM) for a in (sens_maps, direction, residual)))
    core = lax.axis_index("core").astype(jnp.int32).reshape(1)
    packed, core = lax.optimization_barrier((packed, core))
    moved = lax.all_to_all(packed.reshape(devices * ROWS, 1, LANES), axes, 0, 0, tiled=True)
    moved = moved.reshape(devices * ROWS, LANES)
    tables = [jnp.asarray(t) for t in make_tables(sampling.shape[1], sampling.shape[2])]
    swap = [(0, 1), (1, 0)]
    both = jax.ShapeDtypeStruct((2, 3, HALF, LANES), f32)
    first, rest = pl.pallas_call(
        image_kernel,
        out_shape=(jax.ShapeDtypeStruct((2, 2, HALF, LANES), f32), jax.ShapeDtypeStruct((5, HALF, LANES), f32)),
        compiler_params=params,
        name="image",
    )(moved)
    other_rest = lax.ppermute(rest, "core", swap)
    first_mid = pl.pallas_call(
        first_kernel,
        out_shape=jax.ShapeDtypeStruct((2, planes // 2, LANES, 3 * LANES), jnp.bfloat16),
        scratch_shapes=[pltpu.VMEM((planes * HALF, 2 * 3 * LANES), jnp.bfloat16)],
        compiler_params=params,
        name="first",
    )(moved, first, tables[0])
    scalar = pl.BlockSpec(memory_space=pltpu.SMEM)
    own = pl.pallas_call(
        normal_kernel,
        in_specs=[scalar] + [whole] * (5 + len(tables)),
        out_shape=both,
        scratch_shapes=normal_scratch(planes),
        compiler_params=params,
        name="normal",
    )(core, moved, rest, other_rest, first_mid, sampling[0].T, *tables)
    other = lax.ppermute(own, "core", swap)
    chips = devices // 2
    result = pl.pallas_call(
        finish_kernel,
        in_specs=[scalar] + [whole] * 5,
        out_shape=jax.ShapeDtypeStruct((chips, LANES), f32),
        scratch_shapes=[pltpu.VMEM((2 * 3 * HALF, LANES), f32)],
        compiler_params=params,
        name="finish",
    )(core, own, other, first, rest, other_rest)
    home = lax.all_to_all(result.reshape(chips, 1, LANES), chip_axes, 0, 0, tiled=True).reshape(chips, LANES)
    out = jax.ShapeDtypeStruct(direction.shape, f32)
    return tuple(
        pl.pallas_call(update_kernel, out_shape=(out, out, out), compiler_params=params, name="update")(
            home, solution, residual, direction
        )
    )


def solution(mesh):
    split = Mesh(mesh.devices.reshape(mesh.devices.shape[0], EIGHT, -1, 2), ("coil", "line", "place", "core"))
    slab = ("line", "place", "core")
    image = P(None, None, slab, "coil", None)
    in_specs = (image, image, image, P(None, "coil", slab, None, None), P())
    return jax.shard_map(body, mesh=split, in_specs=in_specs, out_specs=(image, image, image), check_vma=False)
```

```python
import math

import jax
import jax.numpy as jnp
import ml_dtypes
import numpy as np
from jax import lax
from jax.experimental import pallas as pl
from jax.experimental.pallas import tpu as pltpu
from jax.sharding import Mesh
from jax.sharding import PartitionSpec as P

damping_weight = 0.5

LANES = 128
ROWS = 7
MESSAGE_IMAGE = 6
HALF = 64
QUARTER = 32
EIGHT = 8
SUMS_AT = 96


def split_pair(table):
    high = table.astype(ml_dtypes.bfloat16)
    low = (table - high.astype(np.float64)).astype(ml_dtypes.bfloat16)
    return np.stack([high, low])


def angles(length):
    index = np.arange(length)
    angle = (index[:, None] * index[None, :] % length) * (2.0 * math.pi / length)
    scale = 1.0 / math.sqrt(length)
    return np.cos(angle) * scale, np.sin(angle) * scale


def make_tables(size_x, size_y):
    cos_y, sin_y = angles(size_y)
    cos_x, sin_x = angles(size_x)
    re_from_re = np.concatenate([cos_y[:, :LANES], -sin_y[:, :LANES], cos_y[:, LANES:], -sin_y[:, LANES:]], axis=1)
    re_from_im = np.concatenate([sin_y[:, :LANES], cos_y[:, :LANES], sin_y[:, LANES:], cos_y[:, LANES:]], axis=1)
    fwd_y = np.concatenate([re_from_re[:LANES], re_from_im[:LANES], re_from_re[LANES:], re_from_im[LANES:]], axis=0)
    order = np.arange(size_x).reshape(EIGHT, -1, 2, 2).transpose(3, 0, 2, 1).reshape(-1)
    fwd_x = np.block([[cos_x[:, order], sin_x[:, order]], [-sin_x[:, order], cos_x[:, order]]])
    fwd_x = fwd_x.reshape(2 * size_x, 2, 2, HALF).transpose(0, 2, 1, 3).reshape(2 * size_x, 2 * size_x)
    return [split_pair(t) for t in (fwd_y, fwd_y.T, fwd_x, fwd_x.T)]


def pack_kernel(maps_hbm, direction_hbm, residual_hbm, out_ref, maps_ref, direction_ref, residual_ref, maps_sem, image_sem):
    cells = maps_ref.shape[4]
    copies = [
        pltpu.make_async_copy(maps_hbm.at[:, core], maps_ref.at[:, core], maps_sem.at[core]) for core in range(2)
    ]
    images = [
        pltpu.make_async_copy(direction_hbm, direction_ref, image_sem.at[0]),
        pltpu.make_async_copy(residual_hbm, residual_ref, image_sem.at[1]),
    ]
    for copy in copies + images:
        copy.start()

    def put(core, slot, block):
        turned = block.T
        for place in range(4):
            rows = pl.ds((core * 4 + place) * ROWS + slot, cells // 4, stride=EIGHT * ROWS)
            out_ref[rows, :] = turned[place * (cells // 4) : (place + 1) * (cells // 4)]

    for core in range(2):
        copies[core].wait()
        for part in range(2):
            for row in range(2):
                put(core, part * 2 + row, maps_ref[part, core, row, :LANES, :])
            put(
                core,
                4 + part,
                jnp.concatenate([maps_ref[part, core, 0, LANES:, :], maps_ref[part, core, 1, LANES:, :]], axis=0),
            )
    for copy in images:
        copy.wait()
    filler = jnp.zeros((LANES - 5 * direction_ref.shape[3], cells), jnp.float32)
    for core in range(2):
        pieces = [direction_ref[0, 0, 0], direction_ref[1, 0, 0], direction_ref[core, 0, 1]]
        pieces += [residual_ref[core, 0, 0], residual_ref[core, 0, 1], filler]
        put(core, MESSAGE_IMAGE, jnp.concatenate(pieces, axis=0))


def lane_index(rows):
    return lax.broadcasted_iota(jnp.int32, (rows, LANES), 1)


def spread(blocks, own, slots):
    lane = lane_index(HALF)
    result = []
    for slot in slots:
        low = jnp.zeros((HALF, LANES), jnp.float32)
        high = jnp.zeros((HALF, LANES), jnp.float32)
        for c, block in enumerate(blocks):
            start = c * own
            moved = pltpu.roll(block, (start - slot * own) % LANES, 1)
            if start < LANES:
                low = jnp.where((lane >= start) & (lane < start + own), moved, low)
            if start + own > LANES:
                at = start - LANES
                high = jnp.where((lane >= at) & (lane < at + own), moved, high)
        result.append((low, high))
    return result


def join_low(first, second):
    return jnp.where(lane_index(HALF) < HALF, first, pltpu.roll(second, HALF, 1))


def join_high(first, second):
    return jnp.where(lane_index(HALF) < HALF, pltpu.roll(first, HALF, 1), second)


def halves(value):
    high = value.astype(jnp.bfloat16)
    low = (value - high.astype(jnp.float32)).astype(jnp.bfloat16)
    return high, low


def dot(a, b):
    return jnp.dot(a, b, preferred_element_type=jnp.float32)


def load_rows(recv_ref, c, slot):
    starts = ((line * EIGHT + c) * EIGHT * ROWS + slot for line in range(EIGHT))
    return jnp.concatenate([recv_ref[pl.ds(start, EIGHT, stride=ROWS), :] for start in starts], axis=0)


def image_kernel(recv_ref, first_ref, rest_ref):
    coils = recv_ref.shape[0] // (ROWS * HALF)
    own = 2 * 96 // coils
    lines = spread([load_rows(recv_ref, c, MESSAGE_IMAGE) for c in range(coils)], own, range(5))
    for part in range(2):
        for index in range(2):
            first_ref[part, index] = lines[part][index]
    for index in range(3):
        rest_ref[index] = lines[2 + index][0]
    rest_ref[3] = join_low(lines[3][1], lines[4][1])
    rest_ref[4] = pltpu.roll(lines[2][1], HALF, 1)


def store_halves(line_ref, c, column, value):
    for term, half in enumerate(halves(value)):
        at = (term * 3 + column) * LANES
        line_ref[c * HALF : (c + 1) * HALF, at : at + LANES] = half


def along_y(line_ref, table_ref):
    twice = jnp.concatenate([table_ref[0], table_ref[0]], axis=0)
    return dot(line_ref[...], twice) + dot(line_ref[:, : 3 * LANES], table_ref[1])


def forward_y(recv_ref, row, image_ref, table_ref, line_ref, mid_ref):
    coils = recv_ref.shape[0] // (ROWS * HALF)
    join = join_high if row else join_low
    for c in range(coils):
        products = []
        for index, slot in enumerate((row, 4)):
            s_re = load_rows(recv_ref, c, slot)
            s_im = load_rows(recv_ref, c, slot + 1 if slot == 4 else slot + 2)
            d_re, d_im = image_ref[0, index], image_ref[1, index]
            products.append((s_re * d_re - s_im * d_im, s_re * d_im + s_im * d_re))
        store_halves(line_ref, c, 0, products[0][0])
        store_halves(line_ref, c, 1, products[0][1])
        store_halves(line_ref, c, 2, join(*products[1]))
    spectra = along_y(line_ref, table_ref)
    for pair in range(coils // 2):
        first, second = (spectra[c * HALF : (c + 1) * HALF] for c in (2 * pair, 2 * pair + 1))
        mixes = first[:, 2 * LANES :], second[:, 2 * LANES :]
        for part, join_part in enumerate((join_low, join_high)):
            columns = (
                first[:, part * LANES : (part + 1) * LANES],
                second[:, part * LANES : (part + 1) * LANES],
                join_part(*mixes),
            )
            for column, value in enumerate(columns):
                for term, half in enumerate(halves(value)):
                    rows = slice(part * HALF, (part + 1) * HALF)
                    mid_ref[term, pair, rows, column * LANES : (column + 1) * LANES] = half


def first_kernel(recv_ref, first_ref, fwd_y_ref, mid_ref, line_ref):
    forward_y(recv_ref, 0, first_ref, fwd_y_ref, line_ref, mid_ref)


def normal_kernel(
    core_ref,
    recv_ref,
    own_rest_ref,
    other_rest_ref,
    first_mid_ref,
    weight_ref,
    fwd_y_ref,
    inv_y_ref,
    fwd_x_ref,
    inv_x_ref,
    total_ref,
    line_ref,
    mid_ref,
    image_ref,
):
    coils = recv_ref.shape[0] // (ROWS * HALF)
    core = core_ref[0]

    def load(c, slot):
        return load_rows(recv_ref, c, slot)

    for part, rest_ref in ((core, own_rest_ref), (1 - core, other_rest_ref)):
        image_ref[part, 0] = rest_ref[0]
        image_ref[part, 1] = rest_ref[4]
    forward_y(recv_ref, 1, image_ref, fwd_y_ref, line_ref.at[1], mid_ref)
    weight_low = weight_ref[:LANES].astype(jnp.float32).T
    weight_high = weight_ref[LANES:].astype(jnp.float32).T
    weight = jnp.concatenate([weight_low, weight_low, jnp.concatenate([weight_high, weight_high], axis=1)], axis=1)
    weight = jnp.concatenate([weight, weight], axis=0)
    for pair in range(coils // 2):
        high, low = (jnp.concatenate([first_mid_ref[term, pair], mid_ref[term, pair]], axis=0) for term in range(2))
        spectra = dot(fwd_x_ref[0], high) + (dot(fwd_x_ref[0], low) + dot(fwd_x_ref[1], high))
        high, low = halves(spectra * weight)
        value = dot(inv_x_ref[0], high) + (dot(inv_x_ref[0], low) + dot(inv_x_ref[1], high))
        for row in range(2):
            re, im = (value[(2 * row + part) * HALF : (2 * row + part + 1) * HALF] for part in range(2))
            mixes = re[:, 2 * LANES :], im[:, 2 * LANES :]
            for index, join in enumerate((join_low, join_high)):
                columns = re, im
                for column, value_part in enumerate(columns):
                    lanes = slice(index * LANES, (index + 1) * LANES)
                    store_halves(line_ref.at[row], 2 * pair + index, column, value_part[:, lanes])
                store_halves(line_ref.at[row], 2 * pair + index, 2, join(*mixes))
    lines = [along_y(line_ref.at[row], inv_y_ref) for row in range(2)]
    for slot in range(3):
        sum_re = jnp.zeros((HALF, LANES), jnp.float32)
        sum_im = jnp.zeros((HALF, LANES), jnp.float32)
        for c in range(coils):
            rows = slice(c * HALF, (c + 1) * HALF)
            s_re = load(c, slot if slot < 2 else 4)
            s_im = load(c, slot + 2 if slot < 2 else 5)
            if slot < 2:
                y_re, y_im = lines[slot][rows, :LANES], lines[slot][rows, LANES : 2 * LANES]
            else:
                first, second = lines[0][rows, 2 * LANES :], lines[1][rows, 2 * LANES :]
                y_re, y_im = join_low(first, second), join_high(first, second)
            sum_re = sum_re + (s_re * y_re + s_im * y_im)
            sum_im = sum_im + (s_re * y_im - s_im * y_re)
        total_ref[0, slot] = sum_re
        total_ref[1, slot] = sum_im


def finish_kernel(core_ref, own_ref, other_ref, first_ref, own_rest_ref, other_rest_ref, out_ref, total_ref):
    core = core_ref[0]
    part_sums = []
    below = lane_index(HALF) < HALF
    for part, rest_ref in ((core, own_rest_ref), (1 - core, other_rest_ref)):
        sums = [jnp.zeros((HALF, LANES), jnp.float32)] * 4
        for slot in range(3):
            residual = rest_ref[slot + 1]
            if slot == 0:
                direction = first_ref[part, 0]
            elif slot == 1:
                direction = rest_ref[0]
            else:
                direction = jnp.where(below, first_ref[part, 1], rest_ref[4])
            image_ap = own_ref[part, slot] + other_ref[part, slot] + damping_weight * direction
            total_ref[pl.ds(pl.multiple_of((part * 3 + slot) * HALF, HALF), HALF), :] = image_ap
            products = (residual * residual, direction * image_ap, residual * image_ap, image_ap * image_ap)
            sums = [a + b for a, b in zip(sums, products)]
        part_sums.append(sums)
    sums = [a + b for a, b in zip(*part_sums)]
    lane = lane_index(QUARTER)
    message = jnp.zeros((QUARTER, LANES), jnp.float32)
    for index, product in enumerate(sums):
        message = jnp.where(lane == SUMS_AT + index, jnp.sum(product), message)
    planes = out_ref.shape[0] // QUARTER
    own = 2 * 96 // planes

    def owned(part, slot):
        base = (part * 3 + slot) * HALF
        first, second = (
            jnp.concatenate(
                [total_ref[pl.ds(base + index * 4 + place, EIGHT, stride=EIGHT), :] for place in range(4)], axis=0
            )
            for index in range(2)
        )
        return jnp.where(core == 0, first, second)

    lines = [[owned(part, slot) for slot in range(3)] for part in range(2)]
    for c in range(planes):
        start = c * own
        block = message
        for part in range(2):
            for row in range(2):
                at = (2 * part + row) * own
                inside = (lane >= at) & (lane < at + own)
                if start < LANES:
                    block = jnp.where(inside, pltpu.roll(lines[part][row], (at - start) % LANES, 1), block)
                if start + own > LANES:
                    moved = pltpu.roll(lines[part][2], (at - (start - LANES + row * HALF)) % LANES, 1)
                    if start < LANES:
                        inside = inside & (lane >= at + LANES - start)
                    block = jnp.where(inside, moved, block)
        for place in range(4):
            out_ref[pl.ds(c * QUARTER + place, EIGHT, stride=4), :] = block[place * EIGHT : (place + 1) * EIGHT]


def update_kernel(
    recv_ref, solution_ref, residual_ref, direction_ref, next_solution_ref, next_residual_ref, next_direction_ref
):
    own = direction_ref.shape[3]
    totals = jnp.sum(recv_ref[...], axis=0, keepdims=True)
    lane = lax.broadcasted_iota(jnp.int32, (1, LANES), 1)

    def pick(index):
        return jnp.sum(jnp.where(lane == SUMS_AT + index, totals, 0.0), axis=1, keepdims=True)

    norm_now, curvature, cross, square = pick(0), pick(1), pick(2), pick(3)
    alpha = norm_now / curvature
    fresh = jnp.maximum(norm_now + alpha * (alpha * square - 2.0 * cross), 0.0)
    beta = fresh / norm_now
    starts = (line * 4 + place for place in range(4) for line in range(EIGHT))
    turned = jnp.concatenate([recv_ref[pl.ds(start, EIGHT, stride=QUARTER), :] for start in starts], axis=0).T
    for part in range(2):
        for row in range(2):
            at = (2 * part + row) * own
            image_ap = turned[at : at + own]
            direction = direction_ref[part, 0, row]
            next_residual = residual_ref[part, 0, row] - alpha * image_ap
            next_solution_ref[part, 0, row] = solution_ref[part, 0, row] + alpha * direction
            next_residual_ref[part, 0, row] = next_residual
            next_direction_ref[part, 0, row] = next_residual + beta * direction


def normal_scratch(planes):
    return [
        pltpu.VMEM((2, planes * HALF, 2 * 3 * LANES), jnp.bfloat16),
        pltpu.VMEM((2, planes // 2, LANES, 3 * LANES), jnp.bfloat16),
        pltpu.VMEM((2, 2, HALF, LANES), jnp.float32),
    ]


def body(solution, residual, direction, sens_maps, sampling):
    chip_axes = ("coil", "line", "place")
    axes = ("line", "coil", "core", "place")
    devices = lax.axis_size(axes)
    planes = lax.axis_size("coil")
    f32 = jnp.float32
    params = pltpu.CompilerParams(vmem_limit_bytes=24 * 1024 * 1024)
    hbm = pl.BlockSpec(memory_space=pl.ANY)
    whole = pl.BlockSpec(memory_space=pltpu.VMEM)
    packed = pl.pallas_call(
        pack_kernel,
        in_specs=[hbm] * 3,
        out_shape=jax.ShapeDtypeStruct((devices * ROWS, LANES), f32),
        scratch_shapes=[pltpu.VMEM(a.shape, f32) for a in (sens_maps, direction, residual)]
        + [pltpu.SemaphoreType.DMA((2,)), pltpu.SemaphoreType.DMA((2,))],
        compiler_params=params,
        name="pack",
    )(*(pltpu.with_memory_space_constraint(a, pltpu.HBM) for a in (sens_maps, direction, residual)))
    core = lax.axis_index("core").astype(jnp.int32).reshape(1)
    packed, core = lax.optimization_barrier((packed, core))
    moved = lax.all_to_all(packed.reshape(devices * ROWS, 1, LANES), axes, 0, 0, tiled=True)
    moved = moved.reshape(devices * ROWS, LANES)
    tables = [jnp.asarray(t) for t in make_tables(sampling.shape[1], sampling.shape[2])]
    swap = [(0, 1), (1, 0)]
    both = jax.ShapeDtypeStruct((2, 3, HALF, LANES), f32)
    first, rest = pl.pallas_call(
        image_kernel,
        out_shape=(jax.ShapeDtypeStruct((2, 2, HALF, LANES), f32), jax.ShapeDtypeStruct((5, HALF, LANES), f32)),
        compiler_params=params,
        name="image",
    )(moved)
    other_rest = lax.ppermute(rest, "core", swap)
    first_mid = pl.pallas_call(
        first_kernel,
        out_shape=jax.ShapeDtypeStruct((2, planes // 2, LANES, 3 * LANES), jnp.bfloat16),
        scratch_shapes=[pltpu.VMEM((planes * HALF, 2 * 3 * LANES), jnp.bfloat16)],
        compiler_params=params,
        name="first",
    )(moved, first, tables[0])
    scalar = pl.BlockSpec(memory_space=pltpu.SMEM)
    own = pl.pallas_call(
        normal_kernel,
        in_specs=[scalar] + [whole] * (5 + len(tables)),
        out_shape=both,
        scratch_shapes=normal_scratch(planes),
        compiler_params=params,
        name="normal",
    )(core, moved, rest, other_rest, first_mid, sampling[0].T, *tables)
    other = lax.ppermute(own, "core", swap)
    chips = devices // 2
    result = pl.pallas_call(
        finish_kernel,
        in_specs=[scalar] + [whole] * 5,
        out_shape=jax.ShapeDtypeStruct((chips, LANES), f32),
        scratch_shapes=[pltpu.VMEM((2 * 3 * HALF, LANES), f32)],
        compiler_params=params,
        name="finish",
    )(core, own, other, first, rest, other_rest)
    home = lax.all_to_all(result.reshape(chips, 1, LANES), chip_axes, 0, 0, tiled=True).reshape(chips, LANES)
    out = jax.ShapeDtypeStruct(direction.shape, f32)
    return tuple(
        pl.pallas_call(update_kernel, out_shape=(out, out, out), compiler_params=params, name="update")(
            home, solution, residual, direction
        )
    )


def solution(mesh):
    split = Mesh(mesh.devices.reshape(mesh.devices.shape[0], EIGHT, -1, 2), ("coil", "line", "place", "core"))
    slab = ("line", "place", "core")
    image = P(None, None, slab, "coil", None)
    in_specs = (image, image, image, P(None, "coil", slab, None, None), P())
    return jax.shard_map(body, mesh=split, in_specs=in_specs, out_specs=(image, image, image), check_vma=False)
```
